512 devices in a mesh: tok: 8 (over x, core), dict: 64 (over z, y).
Axes of the slice: x: 4, y: 4, z: 16, core: 2. Of those that a mesh axis runs over, the one named last changes fastest.
Arguments:
- inputs: bfloat16 [4096, 4608], P('tok', 'dict'), may hold values from -6 to 6
- target: bfloat16 [4096, 4608], P('tok', 'dict'), may hold values from -6 to 6
- enc_weight: bfloat16 [4608, 8192], P(None, 'dict'), may hold values from -0.09375 to 0.09375
- enc_bias: float32 [8192], P('dict'), may hold values from -3 to 3
- dec_weight: bfloat16 [8192, 4608], P('dict'), may hold values from -0.75 to 0.75
- dec_bias: float32 [4608], P('dict'), may hold values from -3 to 3
- skip_weight: bfloat16 [4608, 4608], P(None, 'dict'), may hold values from -0.09375 to 0.09375
- block_ids: int32 [4096, 4], P('tok'), may hold values from 0 to 511, as said below
- slot_lists: int32 [8, 64, 96], P('tok'), may hold values from 0 to 2047, as said below
- slot_counts: int32 [8, 64], P('tok'), may hold values from 0 to 96, as said below
Outputs:
- grad_enc: float32 [4608, 8192], P('tok', 'dict')
- grad_dec: float32 [8192, 4608], P('dict', 'tok')
- grad_skip: float32 [4608, 4608], P('tok', 'dict')
The draws below stay inside these ranges and needn't reach their ends.
Inputs may be any that keep to these rules, and one draw needn't show every extreme that they name: `block_ids`: each token names 4 different blocks of 16 latents. `slot_lists`: A valid slot of list (g, o) holds a code index t * 4 + r of group g (its token t, the token's r-th block); every code of a group stands in exactly one valid slot, in the list of the owner of its block; invalid slots hold 0. `slot_counts`: in every group some list is full.
All inputs are finite; a program needn't handle non-finite values.
Results may differ from the reference program's by a relative error of at most 0.012.
Values may be sent and summed in bfloat16 or wider, within the bound.
No kernel may reach another device: no remote copies, remote signals or barrier semaphores. Data moves between devices by JAX's collectives and lax.ppermute only.
A program may use at most 64 MiB of HBM per device.

```python
import math
import jax
import jax.numpy as jnp
from jax import lax

D = 4608
LAT_DEV = 128
BLK = 16
TOPB = 4
TOK = 512
GROUPS = 8
TOKENS = 4096
LATENTS = 8192
BPO = 8
MEAN = 32
CAP = 96
N_TOK = 8
N_DICT = 64


def group_plan(key):
    key_order, key_items, key_spread, key_base = jax.random.split(key, 4)
    order = jax.random.permutation(key_order, N_DICT).astype(jnp.int32)
    spread = jax.random.randint(key_spread, ((N_DICT - 4) // 2,), 0, MEAN + 1).astype(jnp.int32)
    paired = jnp.stack([MEAN + spread, MEAN - spread], axis=1).reshape(-1)
    head = jnp.array([CAP, 0, 0, MEAN], dtype=jnp.int32)
    by_position = jnp.concatenate([head, paired]).astype(jnp.int32)
    counts = jnp.zeros((N_DICT,), jnp.int32).at[order].set(by_position)
    ends = jnp.cumsum(counts).astype(jnp.int32)
    starts = ends - counts
    items = jax.random.permutation(key_items, TOK * TOPB).astype(jnp.int32)
    slot = jnp.arange(CAP, dtype=jnp.int32)
    place = jnp.clip(starts[:, None] + slot[None, :], 0, TOK * TOPB - 1)
    valid = slot[None, :] < counts[:, None]
    lists = jnp.where(valid, items[place], 0).astype(jnp.int32)
    position = jnp.arange(TOK * TOPB, dtype=jnp.int32)
    owner_at = jnp.sum((position[:, None] >= ends[None, :]).astype(jnp.int32), axis=1)
    owner_of_item = jnp.zeros((TOK * TOPB,), jnp.int32).at[items].set(owner_at)
    base = jax.random.randint(key_base, (TOK, 1), 0, BPO).astype(jnp.int32)
    rounds = jnp.arange(TOPB, dtype=jnp.int32)[None, :]
    local = (base + rounds) % BPO
    blocks = owner_of_item.reshape(TOK, TOPB) * BPO + local
    return (blocks.astype(jnp.int32), lists, counts)


def all_groups(key):
    keys = jax.random.split(jax.random.fold_in(key, 11), GROUPS)
    return jax.vmap(group_plan)(keys)


def draw_block_ids(key, part):
    blocks, lists, counts = all_groups(key)
    return blocks.reshape(TOKENS, TOPB)


def draw_slot_lists(key, part):
    blocks, lists, counts = all_groups(key)
    return lists


def draw_slot_counts(key, part):
    blocks, lists, counts = all_groups(key)
    return counts


def levels(own_key, shape, cuts, smallest, largest):
    loudness, own = 1.0, jax.random.fold_in(own_key, 6)
    for axis_at, shards_of in cuts:
        draws = jnp.exp(jax.random.uniform(jax.random.fold_in(own, axis_at), (shards_of,), jnp.float32, smallest / len(cuts), largest / len(cuts)))
        loudness = loudness * jnp.repeat(draws, shape[axis_at] // shards_of).reshape([-1 if axis == axis_at else 1 for axis in range(len(shape))])
    return loudness


def bell_draw(stream_key, shape, scale, most, cuts=(), kind=jnp.bfloat16):
    values = scale * jax.random.normal(stream_key, shape, jnp.float32)
    if cuts:
        values = values * levels(stream_key, shape, cuts, -0.22, 0.18)
    return jnp.clip(values, -most, most).astype(kind)


def setup_inputs(seed: int = 0) -> dict:
    seeds = jax.random.split(jax.random.key(seed), 11)
    return {
        "inputs": bell_draw(seeds[0], (TOKENS, D), 1.0, 6.0, ((0, 8), (1, 64))),
        "target": bell_draw(seeds[1], (TOKENS, D), 1.0, 6.0, ((0, 8), (1, 64))),
        "enc_weight": bell_draw(seeds[2], (D, LATENTS), D ** -0.5, 0.09375, ((1, 64),)),
        "enc_bias": bell_draw(seeds[3], (LATENTS,), 0.5, 3.0, ((0, 64),), jnp.float32),
        "dec_weight": bell_draw(seeds[4], (LATENTS, D), (BLK * TOPB) ** -0.5, 0.75, ((0, 64),)),
        "dec_bias": bell_draw(seeds[5], (D,), 0.5, 3.0, ((0, 64),), jnp.float32),
        "skip_weight": bell_draw(seeds[6], (D, D), D ** -0.5, 0.09375, ((1, 64),)),
        "block_ids": draw_block_ids(jax.random.fold_in(seeds[10], 71), 0),
        "slot_lists": draw_slot_lists(jax.random.fold_in(seeds[10], 71), 0),
        "slot_counts": draw_slot_counts(jax.random.fold_in(seeds[10], 71), 0),
    }


def gelu_pair(pre):
    factor = math.sqrt(2.0 / math.pi)
    inner = jnp.tanh(factor * (pre + 0.044715 * pre * pre * pre))
    value = 0.5 * pre * (1.0 + inner)
    slope = 0.5 * (1.0 + inner) + 0.5 * pre * (1.0 - inner * inner) * factor * (1.0 + 3.0 * 0.044715 * pre * pre)
    return (value, slope)

def owner_codes(x_group, blocks_flat, slots, count, owner, enc_part, bias_part):
    rows = slots // TOPB
    blocks = blocks_flat[slots]
    latent = owner * LAT_DEV + jnp.arange(LAT_DEV, dtype=jnp.int32)
    valid = jnp.arange(CAP, dtype=jnp.int32) < count
    active = (latent[None, :] // BLK == blocks[:, None]) & valid[:, None]
    picked = x_group[rows]
    pre = jnp.dot(picked, enc_part, preferred_element_type=jnp.float32) + bias_part[None, :]
    value, slope = gelu_pair(pre)
    code = jnp.where(active, value, 0.0).astype(jnp.bfloat16)
    return (rows, active, picked, code, slope)

def reference(inputs, target, enc_weight, enc_bias, dec_weight, dec_bias, skip_weight, block_ids, slot_lists, slot_counts):
    scale = 1.0 / math.sqrt(TOKENS)
    enc_parts = enc_weight.reshape(D, N_DICT, LAT_DEV).transpose(1, 0, 2)
    bias_parts = enc_bias.reshape(N_DICT, LAT_DEV)
    dec_parts = dec_weight.reshape(N_DICT, LAT_DEV, D)
    owners = jnp.arange(N_DICT, dtype=jnp.int32)

    def group_step(carry, group):
        start = (group * TOK).astype(jnp.int32)
        x_group = lax.dynamic_slice_in_dim(inputs, start, TOK, 0)
        y_group = lax.dynamic_slice_in_dim(target, start, TOK, 0)
        blocks_flat = lax.dynamic_slice_in_dim(block_ids, start, TOK, 0).reshape(-1)
        slots_group = slot_lists[group]
        counts_group = slot_counts[group]

        def forward_one(owner):
            rows, active, picked, code, slope = owner_codes(x_group, blocks_flat, slots_group[owner], counts_group[owner], owner, enc_parts[owner], bias_parts[owner])
            return jnp.dot(code, dec_parts[owner], preferred_element_type=jnp.float32).astype(jnp.bfloat16)
        decoded = lax.map(forward_one, owners).reshape(N_DICT * CAP, D)
        rows_all = (slots_group // TOPB).reshape(-1)
        valid_all = (jnp.arange(CAP, dtype=jnp.int32)[None, :] < counts_group[:, None]).reshape(-1)
        placed = jnp.where(valid_all[:, None], decoded.astype(jnp.float32), 0.0)
        recon = jnp.zeros((TOK, D), jnp.float32).at[rows_all].add(placed)
        skip = jnp.dot(x_group, skip_weight, preferred_element_type=jnp.float32)
        err = recon + skip + dec_bias[None, :] - y_group.astype(jnp.float32)
        grad_out = (err * scale).astype(jnp.bfloat16)

        def backward_one(owner):
            rows, active, picked, code, slope = owner_codes(x_group, blocks_flat, slots_group[owner], counts_group[owner], owner, enc_parts[owner], bias_parts[owner])
            grad_rows = grad_out[rows]
            back = jnp.dot(grad_rows, dec_parts[owner].T, preferred_element_type=jnp.float32)
            dpre = jnp.where(active, back * slope, 0.0).astype(jnp.bfloat16)
            enc_term = jnp.dot(picked.T, dpre, preferred_element_type=jnp.float32).astype(jnp.bfloat16)
            dec_term = jnp.dot(code.T, grad_rows, preferred_element_type=jnp.float32).astype(jnp.bfloat16)
            return (enc_term, dec_term)
        enc_terms, dec_terms = lax.map(backward_one, owners)
        skip_term = jnp.dot(x_group.T, grad_out, preferred_element_type=jnp.float32).astype(jnp.bfloat16)
        enc_total, dec_total, skip_total = carry
        return ((enc_total + enc_terms.astype(jnp.float32), dec_total + dec_terms.astype(jnp.float32), skip_total + skip_term.astype(jnp.float32)), None)
    start_carry = (jnp.zeros((N_DICT, D, LAT_DEV), jnp.float32), jnp.zeros((N_DICT, LAT_DEV, D), jnp.float32), jnp.zeros((D, D), jnp.float32))
    totals, unused = lax.scan(group_step, start_carry, jnp.arange(N_TOK, dtype=jnp.int32))
    enc_total, dec_total, skip_total = totals
    grad_enc = enc_total.transpose(1, 0, 2).reshape(D, LATENTS)
    grad_dec = dec_total.reshape(LATENTS, D)
    return (grad_enc, grad_dec, skip_total)
```

```python
import math

import jax
import jax.numpy as jnp
from jax import lax
from jax.sharding import Mesh
from jax.sharding import PartitionSpec as P

BLK = 16
NY = 4
TOK = ("x", "core")
DICT = ("z", "y")
bf16 = jnp.bfloat16
f32 = jnp.float32


def gelu_pair(pre):
    factor = math.sqrt(2.0 / math.pi)
    inner = jnp.tanh(factor * (pre + 0.044715 * pre * pre * pre))
    value = 0.5 * pre * (1.0 + inner)
    slope = 0.5 * (1.0 + inner) + 0.5 * pre * (1.0 - inner * inner) * factor * (
        1.0 + 3.0 * 0.044715 * pre * pre
    )
    return (value, slope)


def ein(spec, a, b):
    return jnp.einsum(spec, a, b, preferred_element_type=f32)


def pick_plan(slots, counts, blocks_t, tok_rows, nb):
    per_token = blocks_t.shape[0]
    cap = slots.shape[1]
    token = slots // per_token
    hot = (token[:, :, None] == jnp.arange(tok_rows, dtype=jnp.int32)).astype(bf16)
    named = ein("rt,nst->nrs", (blocks_t % nb).astype(bf16), hot)
    rank = (slots % per_token)[:, None, :] == jnp.arange(per_token, dtype=jnp.int32)[None, :, None]
    block = jnp.sum(jnp.where(rank, named, 0.0), axis=1)
    valid = jnp.arange(cap, dtype=jnp.int32)[None, :] < counts[:, None]
    mask = (block[:, None, :] == jnp.arange(nb, dtype=f32)[None, :, None]) & valid[:, None, :]
    return hot, mask


def compress(part, plan):
    hot, mask = plan
    n, nb, cap = mask.shape
    rows = ein("nlt,nst->nls", part, hot).reshape(n, nb, BLK, cap)
    return jnp.sum(jnp.where(mask[:, :, None, :], rows, 0.0), axis=1)


def expand(slot_vals, plan):
    hot, mask = plan
    n, nb, cap = mask.shape
    rows = jnp.where(mask[:, :, None, :], slot_vals[:, None, :, :], jnp.zeros((), bf16))
    return ein("nls,nst->nlt", rows.reshape(n, nb * BLK, cap), hot).astype(bf16)


def local(
    inputs,
    target,
    enc_weight,
    enc_bias,
    dec_weight,
    dec_bias,
    skip_weight,
    block_ids,
    slot_lists,
    slot_counts,
):
    tok_rows, fd = inputs.shape
    ld = enc_weight.shape[1]
    nz, ny = lax.axis_size("z"), lax.axis_size("y")
    nx, nc = lax.axis_size("x"), lax.axis_size("core")
    nt = nx * nc
    zl = nz // nt
    nb = ld // BLK
    cap = slot_lists.shape[2]
    zi, yi, ci = lax.axis_index("z"), lax.axis_index("y"), lax.axis_index("core")
    scale = 1.0 / math.sqrt(tok_rows * nt)
    xt = inputs.T
    tt = target.T
    xq = lax.all_gather(xt, "z", axis=0, tiled=True)
    er = lax.all_to_all(enc_weight.reshape(nz, ny, fd, ld), "y", 1, 0).reshape(ny, nz * fd, ld)
    wr = lax.all_to_all(skip_weight.reshape(nz, ny, fd, fd), "y", 1, 0).reshape(ny, nz * fd, fd)
    half = ny * fd // nc
    dt = dec_weight.T.reshape(nz, nc, half, ld)
    dt = lax.dynamic_index_in_dim(dt, ci, 1, keepdims=False)
    dt = lax.all_to_all(dt, "z", 0, 0)
    dd = jnp.concatenate(
        [lax.all_gather(dt[: nz // 2], "core"), lax.all_gather(dt[nz // 2 :], "core")], axis=1
    )
    blocks_t = block_ids.T
    slots = slot_lists[0].reshape(nz, ny, cap)
    counts = slot_counts[0].reshape(nz, ny)
    plan_l = pick_plan(
        lax.dynamic_index_in_dim(slots, yi, 1, keepdims=False),
        lax.dynamic_index_in_dim(counts, yi, 1, keepdims=False),
        blocks_t, tok_rows, nb,
    )
    plan_z = pick_plan(
        lax.dynamic_index_in_dim(slots, zi, 0, keepdims=False),
        lax.dynamic_index_in_dim(counts, zi, 0, keepdims=False),
        blocks_t, tok_rows, nb,
    )
    own_mask = lax.dynamic_index_in_dim(plan_z[1], yi, 0, keepdims=False)
    bias = jnp.sum(jnp.where(own_mask[:, None, :], enc_bias.reshape(nb, BLK)[:, :, None], 0.0), axis=0)
    pre_part = ein("yrl,rt->ylt", er, xq).astype(bf16)
    pre_slots = lax.all_to_all(compress(pre_part, plan_z), "y", 0, 0)
    pre = jnp.sum(pre_slots, axis=0) + bias
    value, slope = gelu_pair(pre)
    code = value.astype(bf16)
    codes_l = lax.all_to_all(jnp.broadcast_to(code[None], (nz,) + code.shape), "z", 0, 0)
    codes_z = lax.all_gather(code, "y")
    dense_l = expand(codes_l, plan_l)
    recon = ein("hzfl,zlt->hft", dd, dense_l).reshape(ny, fd, tok_rows)
    skip = ein("yrc,rt->yct", wr, xq)
    out_part = lax.all_to_all((recon + skip).astype(bf16), "y", 0, 0)
    err = jnp.sum(out_part.astype(f32), axis=0) + dec_bias[:, None] - tt.astype(f32)
    grad = (err * scale).astype(bf16)
    gq = lax.all_gather(grad, "z", axis=0, tiled=True)
    gz = lax.all_gather(grad, "y", axis=0, tiled=True)
    back_part = ein("hzfl,hft->zlt", dd, gz.reshape(nc, half, tok_rows)).astype(bf16)
    back_slots = lax.all_to_all(compress(back_part, plan_l).astype(bf16), "z", 0, 0)
    back = jnp.sum(back_slots.astype(f32), axis=0)
    dpre = (back * slope).astype(bf16)
    dpre_z = expand(lax.all_gather(dpre, "y"), plan_z).reshape(ny * ld, tok_rows)
    code_z = expand(codes_z, plan_z).reshape(ny * ld, tok_rows)
    skip_term = ein("rt,ct->rc", xq, gz).astype(bf16)
    enc_term = ein("rt,lt->rl", xq, dpre_z).astype(bf16)
    dec_term = ein("rt,lt->rl", gq, code_z).astype(bf16)

    def reduce_tok(term):
        c = term.shape[1]
        parts = term.reshape(nx, nc, zl * fd, c)
        mine = lax.dynamic_index_in_dim(parts, ci, 1, keepdims=False)
        theirs = lax.dynamic_index_in_dim(parts, 1 - ci, 1, keepdims=False)
        got = lax.ppermute(theirs, "core", [(0, 1), (1, 0)])
        pair = (mine.astype(f32) + got.astype(f32)).astype(bf16)
        moved = lax.all_to_all(pair, "x", 0, 0)
        return jnp.sum(moved.astype(f32), axis=0)

    def to_owner(total, width):
        t = total.astype(bf16).reshape(zl * fd, ny, width).transpose(1, 0, 2)
        t = lax.all_to_all(t, "y", 0, 0).reshape(ny, zl, fd, width)
        return t.transpose(1, 0, 2, 3).reshape(zl * ny * fd, width).astype(f32)

    grad_skip = to_owner(reduce_tok(skip_term), fd)
    grad_enc = to_owner(reduce_tok(enc_term), ld)
    grad_dec = to_owner(reduce_tok(dec_term), ld).T
    return (grad_enc, grad_dec, grad_skip)


def solution(mesh):
    nt, nd = mesh.devices.shape
    grid = Mesh(mesh.devices.reshape(nt // 2, 2, nd // NY, NY), ("x", "core", "z", "y"))
    in_specs = (
        P(TOK, DICT),
        P(TOK, DICT),
        P(None, DICT),
        P(DICT),
        P(DICT, None),
        P(DICT),
        P(None, DICT),
        P(TOK, None),
        P(TOK, None, None),
        P(TOK, None),
    )
    out_specs = (P(TOK, DICT), P(DICT, TOK), P(TOK, DICT))
    return jax.shard_map(local, mesh=grid, in_specs=in_specs, out_specs=out_specs, check_vma=False)
```

```python
import math

import jax
import jax.numpy as jnp
from jax import lax
from jax.sharding import Mesh
from jax.sharding import PartitionSpec as P

BLK = 16
NY = 4
TOK = ("x", "core")
DICT = ("z", "y")
bf16 = jnp.bfloat16
f32 = jnp.float32


def gelu_pair(pre):
    factor = math.sqrt(2.0 / math.pi)
    inner = jnp.tanh(factor * (pre + 0.044715 * pre * pre * pre))
    value = 0.5 * pre * (1.0 + inner)
    slope = 0.5 * (1.0 + inner) + 0.5 * pre * (1.0 - inner * inner) * factor * (
        1.0 + 3.0 * 0.044715 * pre * pre
    )
    return (value, slope)


def ein(spec, a, b):
    return jnp.einsum(spec, a, b, preferred_element_type=f32)


def pick_plan(slots, counts, blocks_t, tok_rows, nb):
    per_token = blocks_t.shape[0]
    cap = slots.shape[1]
    token = slots // per_token
    hot = (token[:, :, None] == jnp.arange(tok_rows, dtype=jnp.int32)).astype(bf16)
    named = ein("rt,nst->nrs", (blocks_t % nb).astype(bf16), hot)
    rank = (slots % per_token)[:, None, :] == jnp.arange(per_token, dtype=jnp.int32)[None, :, None]
    block = jnp.sum(jnp.where(rank, named, 0.0), axis=1)
    valid = jnp.arange(cap, dtype=jnp.int32)[None, :] < counts[:, None]
    mask = (block[:, None, :] == jnp.arange(nb, dtype=f32)[None, :, None]) & valid[:, None, :]
    return hot, mask


def compress(part, plan):
    hot, mask = plan
    n, nb, cap = mask.shape
    rows = ein("nlt,nst->nls", part, hot).reshape(n, nb, BLK, cap)
    return jnp.sum(jnp.where(mask[:, :, None, :], rows, 0.0), axis=1)


def expand(slot_vals, plan):
    hot, mask = plan
    n, nb, cap = mask.shape
    rows = jnp.where(mask[:, :, None, :], slot_vals[:, None, :, :], jnp.zeros((), bf16))
    return ein("nls,nst->nlt", rows.reshape(n, nb * BLK, cap), hot).astype(bf16)


def local(
    inputs,
    target,
    enc_weight,
    enc_bias,
    dec_weight,
    dec_bias,
    skip_weight,
    block_ids,
    slot_lists,
    slot_counts,
):
    tok_rows, fd = inputs.shape
    ld = enc_weight.shape[1]
    nz, ny = lax.axis_size("z"), lax.axis_size("y")
    nx, nc = lax.axis_size("x"), lax.axis_size("core")
    nt = nx * nc
    zl = nz // nt
    nb = ld // BLK
    cap = slot_lists.shape[2]
    zi, yi, ci = lax.axis_index("z"), lax.axis_index("y"), lax.axis_index("core")
    scale = 1.0 / math.sqrt(tok_rows * nt)
    xt = inputs.T
    tt = target.T

    def share_y(part):
        return lax.all_to_all(jnp.broadcast_to(part[None], (ny,) + part.shape), "y", 0, 0)

    xq = lax.all_gather(xt, "z", axis=0, tiled=True)
    er = lax.all_to_all(enc_weight.reshape(nz, ny, fd, ld), "y", 1, 0).reshape(ny, nz * fd, ld)
    wr = lax.all_to_all(skip_weight.reshape(nz, ny, fd, fd), "y", 1, 0).reshape(ny, nz * fd, fd)
    half = ny * fd // nc
    dt = dec_weight.T.reshape(nz, nc, half, ld)
    dt = lax.dynamic_index_in_dim(dt, ci, 1, keepdims=False)
    dt = lax.all_to_all(dt, "z", 0, 0)
    dd = jnp.concatenate(
        [lax.all_gather(dt[: nz // 2], "core"), lax.all_gather(dt[nz // 2 :], "core")], axis=1
    )
    blocks_t = block_ids.T
    slots = slot_lists[0].reshape(nz, ny, cap)
    counts = slot_counts[0].reshape(nz, ny)
    plan_l = pick_plan(
        lax.dynamic_index_in_dim(slots, yi, 1, keepdims=False),
        lax.dynamic_index_in_dim(counts, yi, 1, keepdims=False),
        blocks_t, tok_rows, nb,
    )
    plan_z = pick_plan(
        lax.dynamic_index_in_dim(slots, zi, 0, keepdims=False),
        lax.dynamic_index_in_dim(counts, zi, 0, keepdims=False),
        blocks_t, tok_rows, nb,
    )
    xq, er, wr, dd, plan_l, plan_z = lax.optimization_barrier((xq, er, wr, dd, plan_l, plan_z))
    own_mask = lax.dynamic_index_in_dim(plan_z[1], yi, 0, keepdims=False)
    bias = jnp.sum(jnp.where(own_mask[:, None, :], enc_bias.reshape(nb, BLK)[:, :, None], 0.0), axis=0)
    pre_part = ein("yrl,rt->ylt", er, xq).astype(bf16)
    pre_slots = lax.all_to_all(compress(pre_part, plan_z), "y", 0, 0)
    pre = jnp.sum(pre_slots, axis=0) + bias
    value, slope = gelu_pair(pre)
    code = value.astype(bf16)
    codes_l = lax.all_to_all(jnp.broadcast_to(code[None], (nz,) + code.shape), "z", 0, 0)
    dense_l = expand(codes_l, plan_l)
    recon = ein("hzfl,zlt->hft", dd, dense_l).reshape(ny, fd, tok_rows)
    skip = ein("yrc,rt->yct", wr, xq)
    out_part = lax.all_to_all((recon + skip).astype(bf16), "y", 0, 0)
    err = jnp.sum(out_part.astype(f32), axis=0) + dec_bias[:, None] - tt.astype(f32)
    grad = (err * scale).astype(bf16)
    gq = lax.all_gather(grad, "z", axis=0, tiled=True)
    gz = share_y(grad).reshape(ny * fd, tok_rows)
    back_part = ein("hzfl,hft->zlt", dd, gz.reshape(nc, half, tok_rows)).astype(bf16)
    back_slots = lax.all_to_all(compress(back_part, plan_l).astype(bf16), "z", 0, 0)
    back = jnp.sum(back_slots.astype(f32), axis=0)
    dpre = (back * slope).astype(bf16)
    slots_z = share_y(jnp.concatenate([dpre, code], axis=0))
    dpre_z = expand(slots_z[:, :BLK], plan_z).reshape(ny * ld, tok_rows)
    code_z = expand(slots_z[:, BLK:], plan_z).reshape(ny * ld, tok_rows)
    first_term = ein("rt,lt->rl", xq, jnp.concatenate([dpre_z, gz], axis=0)).astype(bf16)
    def reduce_tok(term):
        c = term.shape[1]
        parts = term.reshape(nx, nc, zl * fd, c)
        mine = lax.dynamic_index_in_dim(parts, ci, 1, keepdims=False)
        theirs = lax.dynamic_index_in_dim(parts, 1 - ci, 1, keepdims=False)
        got = lax.ppermute(theirs, "core", [(0, 1), (1, 0)])
        pair = (mine.astype(f32) + got.astype(f32)).astype(bf16)
        moved = lax.all_to_all(pair, "x", 0, 0)
        return jnp.sum(moved.astype(f32), axis=0)

    first = reduce_tok(first_term).astype(bf16)
    gq, first = lax.optimization_barrier((gq, first))
    dec_term = ein("rt,lt->rl", gq, code_z).astype(bf16)
    dec = reduce_tok(dec_term).astype(bf16)

    def by_owner(total):
        return total.reshape(zl * fd, ny, total.shape[1] // ny)

    joint = jnp.concatenate(
        [by_owner(first[:, : ny * ld]), by_owner(dec), by_owner(first[:, ny * ld :])], axis=2
    )
    mine = lax.all_to_all(joint.transpose(1, 0, 2), "y", 0, 0).reshape(ny, zl, fd, 2 * ld + fd)
    mine = mine.transpose(1, 0, 2, 3).reshape(zl * ny * fd, 2 * ld + fd).astype(f32)
    grad_enc, grad_dec, grad_skip = mine[:, :ld], mine[:, ld : 2 * ld].T, mine[:, 2 * ld :]
    return (grad_enc, grad_dec, grad_skip)


def solution(mesh):
    nt, nd = mesh.devices.shape
    grid = Mesh(mesh.devices.reshape(nt // 2, 2, nd // NY, NY), ("x", "core", "z", "y"))
    in_specs = (
        P(TOK, DICT),
        P(TOK, DICT),
        P(None, DICT),
        P(DICT),
        P(DICT, None),
        P(DICT),
        P(None, DICT),
        P(TOK, None),
        P(TOK, None, None),
        P(TOK, None),
    )
    out_specs = (P(TOK, DICT), P(DICT, TOK), P(TOK, DICT))
    return jax.shard_map(local, mesh=grid, in_specs=in_specs, out_specs=out_specs, check_vma=False)
```

```python
import math

import jax
import jax.numpy as jnp
from jax import lax
from jax.sharding import Mesh
from jax.sharding import PartitionSpec as P

BLK = 16
NY = 4
TOK = ("x", "core")
Z = ("zh", "zl")
DICT = ("zh", "zl", "y")
bf16 = jnp.bfloat16
f32 = jnp.float32


def gelu_pair(pre):
    factor = math.sqrt(2.0 / math.pi)
    inner = jnp.tanh(factor * (pre + 0.044715 * pre * pre * pre))
    value = 0.5 * pre * (1.0 + inner)
    slope = 0.5 * (1.0 + inner) + 0.5 * pre * (1.0 - inner * inner) * factor * (
        1.0 + 3.0 * 0.044715 * pre * pre
    )
    return (value, slope)


def ein(spec, a, b):
    return jnp.einsum(spec, a, b, preferred_element_type=f32)


def pick_plan(slots, counts, blocks_t, tok_rows, nb):
    per_token = blocks_t.shape[0]
    cap = slots.shape[1]
    token = slots // per_token
    hot = (token[:, :, None] == jnp.arange(tok_rows, dtype=jnp.int32)).astype(bf16)
    named = ein("rt,nst->nrs", (blocks_t % nb).astype(bf16), hot)
    rank = (slots % per_token)[:, None, :] == jnp.arange(per_token, dtype=jnp.int32)[None, :, None]
    block = jnp.sum(jnp.where(rank, named, 0.0), axis=1)
    valid = jnp.arange(cap, dtype=jnp.int32)[None, :] < counts[:, None]
    mask = (block[:, None, :] == jnp.arange(nb, dtype=f32)[None, :, None]) & valid[:, None, :]
    return hot, mask


def compress(part, plan):
    hot, mask = plan
    n, nb, cap = mask.shape
    rows = ein("nlt,nst->nls", part, hot).reshape(n, nb, BLK, cap)
    return jnp.sum(jnp.where(mask[:, :, None, :], rows, 0.0), axis=1)


def expand(slot_vals, plan):
    hot, mask = plan
    n, nb, cap = mask.shape
    rows = jnp.where(mask[:, :, None, :], slot_vals[:, None, :, :], jnp.zeros((), bf16))
    return ein("nls,nst->nlt", rows.reshape(n, nb * BLK, cap), hot).astype(bf16)


def local(
    inputs,
    target,
    enc_weight,
    enc_bias,
    dec_weight,
    dec_bias,
    skip_weight,
    block_ids,
    slot_lists,
    slot_counts,
):
    tok_rows, fd = inputs.shape
    ld = enc_weight.shape[1]
    nz, ny = lax.axis_size(Z), lax.axis_size("y")
    nx, nc = lax.axis_size("x"), lax.axis_size("core")
    nt = nx * nc
    zl = lax.axis_size("zl")
    nb = ld // BLK
    cap = slot_lists.shape[2]
    zi, yi, ci = lax.axis_index(Z), lax.axis_index("y"), lax.axis_index("core")
    scale = 1.0 / math.sqrt(tok_rows * nt)
    xt = inputs.T
    tt = target.T

    def gather_z(part):
        pair = lax.all_gather(part, "zl", axis=0, tiled=True)
        return lax.all_gather(pair, "zh", axis=0, tiled=True)

    def share_y(part):
        return lax.all_to_all(jnp.broadcast_to(part[None], (ny,) + part.shape), "y", 0, 0)

    xq = gather_z(xt)
    er = lax.all_to_all(enc_weight.reshape(nz, ny, fd, ld), "y", 1, 0).reshape(ny, nz * fd, ld)
    wr = lax.all_to_all(skip_weight.reshape(nz, ny, fd, fd), "y", 1, 0).reshape(ny, nz * fd, fd)
    part = ny * fd // nx
    dt = dec_weight.T.reshape(nz, nx, part, ld)
    dt = lax.dynamic_index_in_dim(dt, lax.axis_index("x"), 1, keepdims=False)
    dd = lax.all_gather(lax.all_to_all(dt, Z, 0, 0), "x")
    blocks_t = block_ids.T
    slots = slot_lists[0].reshape(nz, ny, cap)
    counts = slot_counts[0].reshape(nz, ny)
    plan_l = pick_plan(
        lax.dynamic_index_in_dim(slots, yi, 1, keepdims=False),
        lax.dynamic_index_in_dim(counts, yi, 1, keepdims=False),
        blocks_t, tok_rows, nb,
    )
    plan_z = pick_plan(
        lax.dynamic_index_in_dim(slots, zi, 0, keepdims=False),
        lax.dynamic_index_in_dim(counts, zi, 0, keepdims=False),
        blocks_t, tok_rows, nb,
    )
    xq, er, wr, plan_l, plan_z = lax.optimization_barrier((xq, er, wr, plan_l, plan_z))
    own_mask = lax.dynamic_index_in_dim(plan_z[1], yi, 0, keepdims=False)
    bias = jnp.sum(jnp.where(own_mask[:, None, :], enc_bias.reshape(nb, BLK)[:, :, None], 0.0), axis=0)
    pre_part = ein("yrl,rt->ylt", er, xq).astype(bf16)
    pre_slots = lax.all_to_all(compress(pre_part, plan_z), "y", 0, 0)
    pre = jnp.sum(pre_slots, axis=0) + bias
    value, slope = gelu_pair(pre)
    code = value.astype(bf16)
    codes_l = lax.all_to_all(jnp.broadcast_to(code[None], (nz,) + code.shape), Z, 0, 0)
    dense_l = expand(codes_l, plan_l)
    recon = ein("hzfl,zlt->hft", dd, dense_l).reshape(ny, fd, tok_rows)
    skip = ein("yrc,rt->yct", wr, xq)
    out_part = lax.all_to_all((recon + skip).astype(bf16), "y", 0, 0)
    err = jnp.sum(out_part.astype(f32), axis=0) + dec_bias[:, None] - tt.astype(f32)
    grad = (err * scale).astype(bf16)
    gq = gather_z(grad)
    gz = share_y(grad).reshape(ny * fd, tok_rows)
    back_part = ein("hzfl,hft->zlt", dd, gz.reshape(nx, part, tok_rows)).astype(bf16)
    back_slots = lax.all_to_all(compress(back_part, plan_l).astype(bf16), Z, 0, 0)
    back = jnp.sum(back_slots.astype(f32), axis=0)
    dpre = (back * slope).astype(bf16)
    slots_z = share_y(jnp.concatenate([dpre, code], axis=0))
    dpre_z = expand(slots_z[:, :BLK], plan_z).reshape(ny * ld, tok_rows)
    code_z = expand(slots_z[:, BLK:], plan_z).reshape(ny * ld, tok_rows)
    terms = [ein("rt,lt->rl", a, b).astype(bf16) for a, b in ((xq, gz), (xq, dpre_z), (gq, code_z))]

    def rows_of(core):
        split = [t.reshape(nx, nc, zl * fd, t.shape[1]) for t in terms]
        return [lax.dynamic_index_in_dim(t, core, 1, keepdims=False) for t in split]

    got = lax.ppermute(jnp.concatenate(rows_of(1 - ci), axis=2), "core", [(0, 1), (1, 0)])
    pair = (jnp.concatenate(rows_of(ci), axis=2).astype(f32) + got.astype(f32)).astype(bf16)
    total = jnp.sum(lax.all_to_all(pair, "x", 0, 0).astype(f32), axis=0).astype(bf16)
    wide = ny * fd

    def by_owner(total):
        return total.reshape(zl * fd, ny, total.shape[1] // ny)

    joint = jnp.concatenate(
        [by_owner(total[:, wide : wide + ny * ld]), by_owner(total[:, wide + ny * ld :]), by_owner(total[:, :wide])], axis=2
    )
    mine = lax.all_to_all(joint.transpose(1, 0, 2), "y", 0, 0).reshape(ny, zl, fd, 2 * ld + fd)
    mine = mine.transpose(1, 0, 2, 3).reshape(zl * ny * fd, 2 * ld + fd).astype(f32)
    grad_enc, grad_dec, grad_skip = mine[:, :ld], mine[:, ld : 2 * ld].T, mine[:, 2 * ld :]
    return (grad_enc, grad_dec, grad_skip)


def solution(mesh):
    nt, nd = mesh.devices.shape
    shape = (nt // 2, 2, nt, nd // NY // nt, NY)
    grid = Mesh(mesh.devices.reshape(shape), ("x", "core", "zh", "zl", "y"))
    in_specs = (
        P(TOK, DICT),
        P(TOK, DICT),
        P(None, DICT),
        P(DICT),
        P(DICT, None),
        P(DICT),
        P(None, DICT),
        P(TOK, None),
        P(TOK, None, None),
        P(TOK, None),
    )
    out_specs = (P(TOK, DICT), P(DICT, TOK), P(TOK, DICT))
    return jax.shard_map(local, mesh=grid, in_specs=in_specs, out_specs=out_specs, check_vma=False)
```

```python
import math

import jax
import jax.numpy as jnp
from jax import lax
from jax.sharding import Mesh
from jax.sharding import PartitionSpec as P

BLK = 16
NY = 4
TOK = ("x", "core")
Z = ("zh", "zl")
DICT = ("zh", "zl", "y")
bf16 = jnp.bfloat16
f32 = jnp.float32


def gelu_pair(pre):
    factor = math.sqrt(2.0 / math.pi)
    inner = jnp.tanh(factor * (pre + 0.044715 * pre * pre * pre))
    value = 0.5 * pre * (1.0 + inner)
    slope = 0.5 * (1.0 + inner) + 0.5 * pre * (1.0 - inner * inner) * factor * (
        1.0 + 3.0 * 0.044715 * pre * pre
    )
    return (value, slope)


def ein(spec, a, b):
    return jnp.einsum(spec, a, b, preferred_element_type=f32)


def pick_plan(slots, counts, blocks_t, tok_rows, nb):
    per_token = blocks_t.shape[0]
    cap = slots.shape[1]
    token = slots // per_token
    hot = (token[:, :, None] == jnp.arange(tok_rows, dtype=jnp.int32)).astype(bf16)
    named = ein("rt,nst->nrs", (blocks_t % nb).astype(bf16), hot)
    rank = (slots % per_token)[:, None, :] == jnp.arange(per_token, dtype=jnp.int32)[None, :, None]
    block = jnp.sum(jnp.where(rank, named, 0.0), axis=1)
    valid = jnp.arange(cap, dtype=jnp.int32)[None, :] < counts[:, None]
    mask = (block[:, None, :] == jnp.arange(nb, dtype=f32)[None, :, None]) & valid[:, None, :]
    return hot, mask


def compress(part, plan):
    hot, mask = plan
    n, nb, cap = mask.shape
    rows = ein("nlt,nst->nls", part, hot).reshape(n, nb, BLK, cap)
    return jnp.sum(jnp.where(mask[:, :, None, :], rows, 0.0), axis=1)


def expand(slot_vals, plan):
    hot, mask = plan
    n, nb, cap = mask.shape
    rows = jnp.where(mask[:, :, None, :], slot_vals[:, None, :, :], jnp.zeros((), bf16))
    return ein("nls,nst->nlt", rows.reshape(n, nb * BLK, cap), hot).astype(bf16)


def local(
    inputs,
    target,
    enc_weight,
    enc_bias,
    dec_weight,
    dec_bias,
    skip_weight,
    block_ids,
    slot_lists,
    slot_counts,
):
    tok_rows, fd = inputs.shape
    ld = enc_weight.shape[1]
    nz, ny = lax.axis_size(Z), lax.axis_size("y")
    nx, nc = lax.axis_size("x"), lax.axis_size("core")
    nt = nx * nc
    zl = lax.axis_size("zl")
    nb = ld // BLK
    cap = slot_lists.shape[2]
    zi, yi, ci = lax.axis_index(Z), lax.axis_index("y"), lax.axis_index("core")
    scale = 1.0 / math.sqrt(tok_rows * nt)
    xt = inputs.T
    tt = target.T

    def gather_z(part):
        pair = lax.all_gather(part, "zl", axis=0, tiled=True)
        return lax.all_gather(pair, "zh", axis=0, tiled=True)

    def share_y(part):
        return lax.all_to_all(jnp.broadcast_to(part[None], (ny,) + part.shape), "y", 0, 0)

    xq = gather_z(xt)
    er = lax.all_to_all(enc_weight.reshape(nz, ny, fd, ld), "y", 1, 0).reshape(ny, nz * fd, ld)
    part = ny * fd // nx
    xi = lax.axis_index("x")
    dt = dec_weight.T.reshape(nz, nx, part, ld)
    dt = lax.all_to_all(lax.dynamic_index_in_dim(dt, xi, 1, keepdims=False), Z, 0, 0)
    zq = nz // nx
    wt = lax.dynamic_slice_in_dim(skip_weight, xi * zq * ny * fd, zq * ny * fd, 0)
    wt = lax.all_to_all(wt.reshape(zq, ny, fd, fd), "y", 1, 0)
    both = jnp.concatenate([dt, wt.reshape(ny * zq, fd, fd)], axis=2)
    both = lax.all_gather(both, "x")
    dd = both[..., :ld]
    wr = both[..., ld:].reshape(nx, ny, zq * fd, fd)
    blocks_t = block_ids.T
    slots = slot_lists[0].reshape(nz, ny, cap)
    counts = slot_counts[0].reshape(nz, ny)
    plan_l = pick_plan(
        lax.dynamic_index_in_dim(slots, yi, 1, keepdims=False),
        lax.dynamic_index_in_dim(counts, yi, 1, keepdims=False),
        blocks_t, tok_rows, nb,
    )
    plan_z = pick_plan(
        lax.dynamic_index_in_dim(slots, zi, 0, keepdims=False),
        lax.dynamic_index_in_dim(counts, zi, 0, keepdims=False),
        blocks_t, tok_rows, nb,
    )
    xq, er, plan_l, plan_z = lax.optimization_barrier((xq, er, plan_l, plan_z))
    own_mask = lax.dynamic_index_in_dim(plan_z[1], yi, 0, keepdims=False)
    bias = jnp.sum(jnp.where(own_mask[:, None, :], enc_bias.reshape(nb, BLK)[:, :, None], 0.0), axis=0)
    pre_part = ein("yrl,rt->ylt", er, xq).astype(bf16)
    pre_slots = lax.all_to_all(compress(pre_part, plan_z), "y", 0, 0)
    pre = jnp.sum(pre_slots, axis=0) + bias
    value, slope = gelu_pair(pre)
    code = value.astype(bf16)
    codes_l = lax.all_to_all(jnp.broadcast_to(code[None], (nz,) + code.shape), Z, 0, 0)
    dense_l = expand(codes_l, plan_l)
    recon = ein("hzfl,zlt->hft", dd, dense_l).reshape(ny, fd, tok_rows)
    skip = ein("xyrc,xrt->yct", wr, xq.reshape(nx, zq * fd, tok_rows))
    out_part = lax.all_to_all((recon + skip).astype(bf16), "y", 0, 0)
    err = jnp.sum(out_part.astype(f32), axis=0) + dec_bias[:, None] - tt.astype(f32)
    grad = (err * scale).astype(bf16)
    gq = gather_z(grad)
    gz = share_y(grad).reshape(ny * fd, tok_rows)
    back_part = ein("hzfl,hft->zlt", dd, gz.reshape(nx, part, tok_rows)).astype(bf16)
    back_slots = lax.all_to_all(compress(back_part, plan_l).astype(bf16), Z, 0, 0)
    back = jnp.sum(back_slots.astype(f32), axis=0)
    dpre = (back * slope).astype(bf16)
    slots_z = share_y(jnp.concatenate([dpre, code], axis=0))
    dpre_z = expand(slots_z[:, :BLK], plan_z).reshape(ny * ld, tok_rows)
    code_z = expand(slots_z[:, BLK:], plan_z).reshape(ny * ld, tok_rows)
    def rows_of(core, rows):
        split = rows.reshape(nx, nc, zl * fd, tok_rows)
        return lax.dynamic_index_in_dim(split, core, 1, keepdims=False)

    def terms_of(core, gq):
        xc, gc = rows_of(core, xq), rows_of(core, gq)
        pairs = ((xc, gz), (xc, dpre_z), (gc, code_z))
        return jnp.concatenate([ein("art,lt->arl", a, b).astype(bf16) for a, b in pairs], axis=2)

    got = lax.ppermute(terms_of(1 - ci, gq), "core", [(0, 1), (1, 0)])
    pair = (terms_of(ci, gq).astype(f32) + got.astype(f32)).astype(bf16)
    total = jnp.sum(lax.all_to_all(pair, "x", 0, 0).astype(f32), axis=0).astype(bf16)
    wide = ny * fd

    def by_owner(total):
        return total.reshape(zl * fd, ny, total.shape[1] // ny)

    joint = jnp.concatenate(
        [by_owner(total[:, wide : wide + ny * ld]), by_owner(total[:, wide + ny * ld :]), by_owner(total[:, :wide])], axis=2
    )
    mine = lax.all_to_all(joint.transpose(1, 0, 2), "y", 0, 0).reshape(ny, zl, fd, 2 * ld + fd)
    mine = mine.transpose(1, 0, 2, 3).reshape(zl * ny * fd, 2 * ld + fd).astype(f32)
    grad_enc, grad_dec, grad_skip = mine[:, :ld], mine[:, ld : 2 * ld].T, mine[:, 2 * ld :]
    return (grad_enc, grad_dec, grad_skip)


def solution(mesh):
    nt, nd = mesh.devices.shape
    shape = (nt // 2, 2, nt, nd // NY // nt, NY)
    grid = Mesh(mesh.devices.reshape(shape), ("x", "core", "zh", "zl", "y"))
    in_specs = (
        P(TOK, DICT),
        P(TOK, DICT),
        P(None, DICT),
        P(DICT),
        P(DICT, None),
        P(DICT),
        P(None, DICT),
        P(TOK, None),
        P(TOK, None, None),
        P(TOK, None),
    )
    out_specs = (P(TOK, DICT), P(DICT, TOK), P(TOK, DICT))
    return jax.shard_map(local, mesh=grid, in_specs=in_specs, out_specs=out_specs, check_vma=False)
```

```python
import math

import jax
import jax.numpy as jnp
from jax import lax
from jax.experimental import pallas as pl
from jax.experimental.pallas import tpu as pltpu
from jax.sharding import Mesh
from jax.sharding import PartitionSpec as P

BLK = 16
NY = 4
INTERPRET = False
TOK = ("x", "core")
Z = ("zh", "zl")
DICT = ("zh", "zl", "y")
bf16 = jnp.bfloat16
f32 = jnp.float32


def gelu_pair(pre):
    factor = math.sqrt(2.0 / math.pi)
    inner = jnp.tanh(factor * (pre + 0.044715 * pre * pre * pre))
    value = 0.5 * pre * (1.0 + inner)
    slope = 0.5 * (1.0 + inner) + 0.5 * pre * (1.0 - inner * inner) * factor * (
        1.0 + 3.0 * 0.044715 * pre * pre
    )
    return (value, slope)


def ein(spec, a, b):
    return jnp.einsum(spec, a, b, preferred_element_type=f32)


def pick_plan(slots, counts, blocks_t, tok_rows, nb):
    per_token = blocks_t.shape[0]
    cap = slots.shape[1]
    token = slots // per_token
    hot = (token[:, :, None] == jnp.arange(tok_rows, dtype=jnp.int32)).astype(bf16)
    named = ein("rt,nst->nrs", (blocks_t % nb).astype(bf16), hot)
    rank = (slots % per_token)[:, None, :] == jnp.arange(per_token, dtype=jnp.int32)[None, :, None]
    block = jnp.sum(jnp.where(rank, named, 0.0), axis=1)
    valid = jnp.arange(cap, dtype=jnp.int32)[None, :] < counts[:, None]
    mask = (block[:, None, :] == jnp.arange(nb, dtype=f32)[None, :, None]) & valid[:, None, :]
    return hot, mask


def compress(part, plan):
    hot, mask = plan
    n, nb, cap = mask.shape
    rows = ein("nlt,nst->nls", part, hot).reshape(n, nb, BLK, cap)
    return jnp.sum(jnp.where(mask[:, :, None, :], rows, 0.0), axis=1)


def expand(slot_vals, plan):
    hot, mask = plan
    n, nb, cap = mask.shape
    rows = jnp.where(mask[:, :, None, :], slot_vals[:, None, :, :], jnp.zeros((), bf16))
    return ein("nls,nst->nlt", rows.reshape(n, nb * BLK, cap), hot).astype(bf16)


def grad_block(core, operands, got):
    xq, gq, dpre, code, grad = operands
    nx, _, rows, toks = xq.shape
    lat, wide = dpre.shape[0], grad.shape[0]
    cols = 2 * lat + wide

    def body(core_ref, x_ref, g_ref, dpre_ref, code_ref, grad_ref, *rest):
        out_ref = rest[-1]

        def put(a, b, lo, hi):
            part = lax.dot_general(a, b, (((1,), (1,)), ((), ())), preferred_element_type=f32)
            if got is not None:
                part = part + rest[0][0, :, lo:hi].astype(f32)
            out_ref[0, :, lo:hi] = part.astype(bf16)

        x, g = x_ref[0, 0], g_ref[0, 0]
        put(x, dpre_ref[...], 0, lat)
        put(g, code_ref[...], lat, 2 * lat)
        put(x, grad_ref[...], 2 * lat, cols)

    block = pl.BlockSpec((1, 1, rows, toks), lambda i, c: (i, c[0], 0, 0))
    joint = pl.BlockSpec((1, rows, cols), lambda i, c: (i, 0, 0))
    whole = [pl.BlockSpec((n, toks), lambda i, c: (0, 0)) for n in (lat, lat, wide)]
    extra = () if got is None else (got,)
    return pl.pallas_call(
        body,
        grid_spec=pltpu.PrefetchScalarGridSpec(
            num_scalar_prefetch=1,
            grid=(nx,),
            in_specs=[block, block, *whole] + [joint] * len(extra),
            out_specs=joint,
        ),
        out_shape=jax.ShapeDtypeStruct((nx, rows, cols), bf16),
        interpret=INTERPRET,
    )(core.reshape(1).astype(jnp.int32), xq, gq, dpre, code, grad, *extra)


def local(
    inputs,
    target,
    enc_weight,
    enc_bias,
    dec_weight,
    dec_bias,
    skip_weight,
    block_ids,
    slot_lists,
    slot_counts,
):
    tok_rows, fd = inputs.shape
    ld = enc_weight.shape[1]
    nz, ny = lax.axis_size(Z), lax.axis_size("y")
    nx, nc = lax.axis_size("x"), lax.axis_size("core")
    nt = nx * nc
    zl = lax.axis_size("zl")
    nb = ld // BLK
    cap = slot_lists.shape[2]
    zi, yi, ci = lax.axis_index(Z), lax.axis_index("y"), lax.axis_index("core")
    scale = 1.0 / math.sqrt(tok_rows * nt)
    xt = inputs.T
    tt = target.T

    def gather_z(part):
        pair = lax.all_gather(part, "zl", axis=0, tiled=True)
        return lax.all_gather(pair, "zh", axis=0, tiled=True)

    def share_y(part):
        return lax.all_to_all(jnp.broadcast_to(part[None], (ny,) + part.shape), "y", 0, 0)

    xq = gather_z(xt)
    er = lax.all_to_all(enc_weight.reshape(nz, ny, fd, ld), "y", 1, 0).reshape(ny, nz * fd, ld)
    zc = nz // nc
    wt = lax.dynamic_slice_in_dim(skip_weight, ci * zc * ny * fd, zc * ny * fd, 0)
    wt = lax.all_to_all(wt.reshape(zc, ny, fd, fd), "y", 1, 0).reshape(ny, zc * fd, fd)
    wr = lax.all_gather(wt, "core")
    part = ny * fd // nx
    dt = dec_weight.T.reshape(nz, nx, part, ld)
    dt = lax.dynamic_index_in_dim(dt, lax.axis_index("x"), 1, keepdims=False)
    dd = lax.all_gather(lax.all_to_all(dt, Z, 0, 0), "x")
    blocks_t = block_ids.T
    slots = slot_lists[0].reshape(nz, ny, cap)
    counts = slot_counts[0].reshape(nz, ny)
    plan_l = pick_plan(
        lax.dynamic_index_in_dim(slots, yi, 1, keepdims=False),
        lax.dynamic_index_in_dim(counts, yi, 1, keepdims=False),
        blocks_t, tok_rows, nb,
    )
    plan_z = pick_plan(
        lax.dynamic_index_in_dim(slots, zi, 0, keepdims=False),
        lax.dynamic_index_in_dim(counts, zi, 0, keepdims=False),
        blocks_t, tok_rows, nb,
    )
    xq, er, wr, plan_l, plan_z = lax.optimization_barrier((xq, er, wr, plan_l, plan_z))
    own_mask = lax.dynamic_index_in_dim(plan_z[1], yi, 0, keepdims=False)
    bias = jnp.sum(jnp.where(own_mask[:, None, :], enc_bias.reshape(nb, BLK)[:, :, None], 0.0), axis=0)
    pre_part = ein("yrl,rt->ylt", er, xq).astype(bf16)
    pre_slots = lax.all_to_all(compress(pre_part, plan_z), "y", 0, 0)
    pre = jnp.sum(pre_slots, axis=0) + bias
    value, slope = gelu_pair(pre)
    code = value.astype(bf16)
    codes_l = lax.all_to_all(jnp.broadcast_to(code[None], (nz,) + code.shape), Z, 0, 0)
    dense_l = expand(codes_l, plan_l)
    recon = ein("hzfl,zlt->hft", dd, dense_l).reshape(ny, fd, tok_rows)
    skip = ein("ayrc,art->yct", wr, xq.reshape(nc, zc * fd, tok_rows))
    out_part = lax.all_to_all((recon + skip).astype(bf16), "y", 0, 0)
    err = jnp.sum(out_part.astype(f32), axis=0) + dec_bias[:, None] - tt.astype(f32)
    grad = (err * scale).astype(bf16)
    gq = gather_z(grad)
    gz = share_y(grad).reshape(ny * fd, tok_rows)
    back_part = ein("hzfl,hft->zlt", dd, gz.reshape(nx, part, tok_rows)).astype(bf16)
    back_slots = lax.all_to_all(compress(back_part, plan_l).astype(bf16), Z, 0, 0)
    back = jnp.sum(back_slots.astype(f32), axis=0)
    dpre = (back * slope).astype(bf16)
    slots_z = share_y(jnp.concatenate([dpre, code], axis=0))
    dpre_z = expand(slots_z[:, :BLK], plan_z).reshape(ny * ld, tok_rows)
    code_z = expand(slots_z[:, BLK:], plan_z).reshape(ny * ld, tok_rows)
    blocks = (nx, nc, zl * fd, tok_rows)
    operands = (xq.reshape(blocks), gq.reshape(blocks), dpre_z, code_z, gz)
    theirs = grad_block(1 - ci, operands, None)
    got = lax.ppermute(theirs, "core", [(0, 1), (1, 0)])
    pair = grad_block(ci, operands, got)
    total = jnp.sum(lax.all_to_all(pair, "x", 0, 0).astype(f32), axis=0).astype(bf16)
    lat = ny * ld

    def by_owner(total):
        return total.reshape(zl * fd, ny, total.shape[1] // ny)

    joint = jnp.concatenate(
        [by_owner(total[:, :lat]), by_owner(total[:, lat : 2 * lat]), by_owner(total[:, 2 * lat :])], axis=2
    )
    mine = lax.all_to_all(joint.transpose(1, 0, 2), "y", 0, 0).reshape(ny, zl, fd, 2 * ld + fd)
    mine = mine.transpose(1, 0, 2, 3).reshape(zl * ny * fd, 2 * ld + fd).astype(f32)
    grad_enc, grad_dec, grad_skip = mine[:, :ld], mine[:, ld : 2 * ld].T, mine[:, 2 * ld :]
    return (grad_enc, grad_dec, grad_skip)


def solution(mesh):
    nt, nd = mesh.devices.shape
    shape = (nt // 2, 2, nt, nd // NY // nt, NY)
    grid = Mesh(mesh.devices.reshape(shape), ("x", "core", "zh", "zl", "y"))
    in_specs = (
        P(TOK, DICT),
        P(TOK, DICT),
        P(None, DICT),
        P(DICT),
        P(DICT, None),
        P(DICT),
        P(None, DICT),
        P(TOK, None),
        P(TOK, None, None),
        P(TOK, None),
    )
    out_specs = (P(TOK, DICT), P(DICT, TOK), P(TOK, DICT))
    return jax.shard_map(local, mesh=grid, in_specs=in_specs, out_specs=out_specs, check_vma=False)
```

```python
import math

import jax
import jax.numpy as jnp
from jax import lax
from jax.experimental import pallas as pl
from jax.experimental.pallas import tpu as pltpu
from jax.sharding import Mesh
from jax.sharding import PartitionSpec as P

BLK = 16
NY = 4
INTERPRET = False
TOK = ("x", "core")
Z = ("zh", "zl")
DICT = ("zh", "zl", "y")
bf16 = jnp.bfloat16
f32 = jnp.float32


def gelu_pair(pre):
    factor = math.sqrt(2.0 / math.pi)
    inner = jnp.tanh(factor * (pre + 0.044715 * pre * pre * pre))
    value = 0.5 * pre * (1.0 + inner)
    slope = 0.5 * (1.0 + inner) + 0.5 * pre * (1.0 - inner * inner) * factor * (
        1.0 + 3.0 * 0.044715 * pre * pre
    )
    return (value, slope)


def ein(spec, a, b):
    return jnp.einsum(spec, a, b, preferred_element_type=f32)


def pick_plan(slots, counts, blocks_t, tok_rows, nb):
    per_token = blocks_t.shape[0]
    cap = slots.shape[1]
    token = slots // per_token
    hot = (token[:, :, None] == jnp.arange(tok_rows, dtype=jnp.int32)).astype(bf16)
    named = ein("rt,nst->nrs", (blocks_t % nb).astype(bf16), hot)
    rank = (slots % per_token)[:, None, :] == jnp.arange(per_token, dtype=jnp.int32)[None, :, None]
    block = jnp.sum(jnp.where(rank, named, 0.0), axis=1)
    valid = jnp.arange(cap, dtype=jnp.int32)[None, :] < counts[:, None]
    mask = (block[:, None, :] == jnp.arange(nb, dtype=f32)[None, :, None]) & valid[:, None, :]
    return hot, mask


def compress(part, plan):
    hot, mask = plan
    n, nb, cap = mask.shape
    rows = ein("nlt,nst->nls", part, hot).reshape(n, nb, BLK, cap)
    return jnp.sum(jnp.where(mask[:, :, None, :], rows, 0.0), axis=1)


def expand(slot_vals, plan):
    hot, mask = plan
    n, nb, cap = mask.shape
    rows = jnp.where(mask[:, :, None, :], slot_vals[:, None, :, :], jnp.zeros((), bf16))
    return ein("nls,nst->nlt", rows.reshape(n, nb * BLK, cap), hot).astype(bf16)


def grad_block(core, operands, got):
    xq, gq, dpre, code, grad = operands
    nx, _, rows, toks = xq.shape
    lat, wide = dpre.shape[0], grad.shape[0]
    cols = 2 * lat + wide

    def body(core_ref, x_ref, g_ref, dpre_ref, code_ref, grad_ref, *rest):
        out_ref = rest[-1]
        core_at = core_ref[0]

        def put(a, b, lo, hi):
            part = lax.dot_general(a, b, (((1,), (1,)), ((), ())), preferred_element_type=f32)
            part = part.reshape(nx, rows, hi - lo)
            if got is not None:
                part = part + rest[0][:, :, lo:hi].astype(f32)
            out_ref[:, :, lo:hi] = part.astype(bf16)

        x = x_ref[:, core_at].reshape(nx * rows, toks)
        put(x, grad_ref[...], 2 * lat, cols)
        put(x, dpre_ref[...], 0, lat)
        g = g_ref[:, core_at].reshape(nx * rows, toks)
        put(g, code_ref[...], lat, 2 * lat)

    extra = () if got is None else (got,)
    vmem = pl.BlockSpec(memory_space=pltpu.VMEM)
    return pl.pallas_call(
        body,
        in_specs=[pl.BlockSpec(memory_space=pltpu.SMEM)] + [vmem] * (5 + len(extra)),
        out_specs=vmem,
        out_shape=jax.ShapeDtypeStruct((nx, rows, cols), bf16),
        interpret=INTERPRET,
    )(core.reshape(1).astype(jnp.int32), xq, gq, dpre, code, grad, *extra)


def local(
    inputs,
    target,
    enc_weight,
    enc_bias,
    dec_weight,
    dec_bias,
    skip_weight,
    block_ids,
    slot_lists,
    slot_counts,
):
    tok_rows, fd = inputs.shape
    ld = enc_weight.shape[1]
    nz, ny = lax.axis_size(Z), lax.axis_size("y")
    nx, nc = lax.axis_size("x"), lax.axis_size("core")
    nt = nx * nc
    zl = lax.axis_size("zl")
    nb = ld // BLK
    cap = slot_lists.shape[2]
    zi, yi, ci = lax.axis_index(Z), lax.axis_index("y"), lax.axis_index("core")
    scale = 1.0 / math.sqrt(tok_rows * nt)
    xt = inputs.T
    tt = target.T

    def gather_z(part):
        pair = lax.all_gather(part, "zl", axis=0, tiled=True)
        return lax.all_gather(pair, "zh", axis=0, tiled=True)

    def share_y(part):
        return lax.all_to_all(jnp.broadcast_to(part[None], (ny,) + part.shape), "y", 0, 0)

    xq = gather_z(xt)
    er = lax.all_to_all(enc_weight.reshape(nz, ny, fd, ld), "y", 1, 0).reshape(ny, nz * fd, ld)
    zc = nz // nc
    wt = lax.dynamic_slice_in_dim(skip_weight, ci * zc * ny * fd, zc * ny * fd, 0)
    wt = lax.all_to_all(wt.reshape(zc, ny, fd, fd), "y", 1, 0).reshape(ny, zc * fd, fd)
    wr = lax.all_gather(wt, "core")
    lt = ld // nt
    dt = lax.dynamic_slice_in_dim(dec_weight, lax.axis_index(TOK) * lt, lt, 0)
    dt = lax.all_to_all(dt.reshape(lt, nz, ny * fd).transpose(1, 0, 2), Z, 0, 0)
    dd = lax.all_gather(dt, TOK).transpose(1, 0, 2, 3).reshape(nz, ld, ny * fd)
    blocks_t = block_ids.T
    slots = slot_lists[0].reshape(nz, ny, cap)
    counts = slot_counts[0].reshape(nz, ny)
    plan_l = pick_plan(
        lax.dynamic_index_in_dim(slots, yi, 1, keepdims=False),
        lax.dynamic_index_in_dim(counts, yi, 1, keepdims=False),
        blocks_t, tok_rows, nb,
    )
    plan_z = pick_plan(
        lax.dynamic_index_in_dim(slots, zi, 0, keepdims=False),
        lax.dynamic_index_in_dim(counts, zi, 0, keepdims=False),
        blocks_t, tok_rows, nb,
    )
    xq, er, wr, plan_l, plan_z = lax.optimization_barrier((xq, er, wr, plan_l, plan_z))
    own_mask = lax.dynamic_index_in_dim(plan_z[1], yi, 0, keepdims=False)
    bias = jnp.sum(jnp.where(own_mask[:, None, :], enc_bias.reshape(nb, BLK)[:, :, None], 0.0), axis=0)
    pre_part = ein("yrl,rt->ylt", er, xq).astype(bf16)
    pre_slots = lax.all_to_all(compress(pre_part, plan_z), "y", 0, 0)
    pre = jnp.sum(pre_slots, axis=0) + bias
    value, slope = gelu_pair(pre)
    code = value.astype(bf16)
    codes_l = lax.all_to_all(jnp.broadcast_to(code[None], (nz,) + code.shape), Z, 0, 0)
    dense_l = expand(codes_l, plan_l)
    recon = ein("zlf,zlt->ft", dd, dense_l).reshape(ny, fd, tok_rows)
    skip = ein("ayrc,art->yct", wr, xq.reshape(nc, zc * fd, tok_rows))
    out_part = lax.all_to_all((recon + skip).astype(bf16), "y", 0, 0)
    err = jnp.sum(out_part.astype(f32), axis=0) + dec_bias[:, None] - tt.astype(f32)
    grad = (err * scale).astype(bf16)
    gq = gather_z(grad)
    gz = share_y(grad).reshape(ny * fd, tok_rows)
    back_part = ein("zlf,ft->zlt", dd, gz).astype(bf16)
    back_slots = lax.all_to_all(compress(back_part, plan_l).astype(bf16), Z, 0, 0)
    back = jnp.sum(back_slots.astype(f32), axis=0)
    dpre = (back * slope).astype(bf16)
    slots_z = share_y(jnp.concatenate([dpre, code], axis=0))
    dpre_z = expand(slots_z[:, :BLK], plan_z).reshape(ny * ld, tok_rows)
    code_z = expand(slots_z[:, BLK:], plan_z).reshape(ny * ld, tok_rows)
    blocks = (nx, nc, zl * fd, tok_rows)
    operands = (xq.reshape(blocks), gq.reshape(blocks), dpre_z, code_z, gz)
    theirs = grad_block(1 - ci, operands, None)
    got = lax.ppermute(theirs, "core", [(0, 1), (1, 0)])
    pair = grad_block(ci, operands, got)
    total = jnp.sum(lax.all_to_all(pair, "x", 0, 0).astype(f32), axis=0).astype(bf16)
    lat = ny * ld

    def by_owner(total):
        return total.reshape(zl * fd, ny, total.shape[1] // ny)

    joint = jnp.concatenate(
        [by_owner(total[:, :lat]), by_owner(total[:, lat : 2 * lat]), by_owner(total[:, 2 * lat :])], axis=2
    )
    mine = lax.all_to_all(joint.transpose(1, 0, 2), "y", 0, 0).reshape(ny, zl, fd, 2 * ld + fd)
    mine = mine.transpose(1, 0, 2, 3).reshape(zl * ny * fd, 2 * ld + fd).astype(f32)
    grad_enc, grad_dec, grad_skip = mine[:, :ld], mine[:, ld : 2 * ld].T, mine[:, 2 * ld :]
    return (grad_enc, grad_dec, grad_skip)


def solution(mesh):
    nt, nd = mesh.devices.shape
    shape = (nt // 2, 2, nt, nd // NY // nt, NY)
    grid = Mesh(mesh.devices.reshape(shape), ("x", "core", "zh", "zl", "y"))
    in_specs = (
        P(TOK, DICT),
        P(TOK, DICT),
        P(None, DICT),
        P(DICT),
        P(DICT, None),
        P(DICT),
        P(None, DICT),
        P(TOK, None),
        P(TOK, None, None),
        P(TOK, None),
    )
    out_specs = (P(TOK, DICT), P(DICT, TOK), P(TOK, DICT))
    return jax.shard_map(local, mesh=grid, in_specs=in_specs, out_specs=out_specs, check_vma=False)
```

```python
import math

import jax
import jax.numpy as jnp
from jax import lax
from jax.experimental import pallas as pl
from jax.experimental.pallas import tpu as pltpu
from jax.sharding import Mesh
from jax.sharding import PartitionSpec as P

BLK = 16
NY = 4
INTERPRET = False
TOK = ("x", "core")
Z = ("zh", "zl")
DICT = ("zh", "zl", "y")
bf16 = jnp.bfloat16
f32 = jnp.float32


def gelu_pair(pre):
    factor = math.sqrt(2.0 / math.pi)
    inner = jnp.tanh(factor * (pre + 0.044715 * pre * pre * pre))
    value = 0.5 * pre * (1.0 + inner)
    slope = 0.5 * (1.0 + inner) + 0.5 * pre * (1.0 - inner * inner) * factor * (
        1.0 + 3.0 * 0.044715 * pre * pre
    )
    return (value, slope)


def ein(spec, a, b):
    return jnp.einsum(spec, a, b, preferred_element_type=f32)


def pick_plan(slots, counts, blocks_t, tok_rows, nb):
    per_token = blocks_t.shape[0]
    cap = slots.shape[1]
    token = slots // per_token
    hot = (token[:, :, None] == jnp.arange(tok_rows, dtype=jnp.int32)).astype(bf16)
    named = ein("rt,nst->nrs", (blocks_t % nb).astype(bf16), hot)
    rank = (slots % per_token)[:, None, :] == jnp.arange(per_token, dtype=jnp.int32)[None, :, None]
    block = jnp.sum(jnp.where(rank, named, 0.0), axis=1)
    valid = jnp.arange(cap, dtype=jnp.int32)[None, :] < counts[:, None]
    mask = (block[:, None, :] == jnp.arange(nb, dtype=f32)[None, :, None]) & valid[:, None, :]
    return hot, mask


def compress(part, plan):
    hot, mask = plan
    n, nb, cap = mask.shape
    rows = ein("nlt,nst->nls", part, hot).reshape(n, nb, BLK, cap)
    return jnp.sum(jnp.where(mask[:, :, None, :], rows, 0.0), axis=1)


def expand(slot_vals, plan):
    hot, mask = plan
    n, nb, cap = mask.shape
    rows = jnp.where(mask[:, :, None, :], slot_vals[:, None, :, :], jnp.zeros((), bf16))
    return ein("nls,nst->nlt", rows.reshape(n, nb * BLK, cap), hot).astype(bf16)


def contract(a, b, dim_a, dim_b):
    return lax.dot_general(a, b, (((dim_a,), (dim_b,)), ((), ())), preferred_element_type=f32)


def decode_slots(codes, named, hot, dec, skip, feats):
    n, lat, cap = named.shape
    toks, wide = hot.shape[2], dec.shape[3]
    parts, _, rows = skip.shape

    def body(codes_ref, named_ref, hot_ref, dec_ref, skip_ref, feats_ref, out_ref, slots_ref):
        for z in range(n):
            code = jnp.concatenate([codes_ref[z]] * (lat // BLK), axis=0) * named_ref[z]
            slots_ref[z] = contract(code, dec_ref[:, z].reshape(lat, wide), 0, 0).astype(bf16)
        total = contract(slots_ref[...].reshape(n * cap, wide), hot_ref[...].reshape(n * cap, toks), 0, 0)
        for k in range(parts):
            total = total + contract(skip_ref[k], feats_ref[k * rows : (k + 1) * rows], 1, 0)
        out_ref[...] = total.astype(bf16)

    vmem = pl.BlockSpec(memory_space=pltpu.VMEM)
    return pl.pallas_call(
        body,
        in_specs=[vmem] * 6,
        out_specs=vmem,
        out_shape=jax.ShapeDtypeStruct((wide, toks), bf16),
        scratch_shapes=[pltpu.VMEM((n, cap, wide), bf16)],
        interpret=INTERPRET,
    )(codes, named, hot, dec, skip, feats)


def back_to_slots(grad, named, hot, dec):
    n, lat, cap = named.shape
    toks, wide = hot.shape[2], dec.shape[3]

    def body(grad_ref, named_ref, hot_ref, dec_ref, out_ref):
        picked = contract(hot_ref[...].reshape(n * cap, toks), grad_ref[...], 1, 1).astype(bf16)
        for z in range(n):
            rows = contract(dec_ref[:, z].reshape(lat, wide), picked[z * cap : (z + 1) * cap], 1, 1)
            rows = rows * named_ref[z].astype(f32)
            total = rows[:BLK]
            for b in range(1, lat // BLK):
                total = total + rows[b * BLK : (b + 1) * BLK]
            out_ref[z] = total.astype(bf16)

    vmem = pl.BlockSpec(memory_space=pltpu.VMEM)
    return pl.pallas_call(
        body,
        in_specs=[vmem] * 4,
        out_specs=vmem,
        out_shape=jax.ShapeDtypeStruct((n, BLK, cap), bf16),
        interpret=INTERPRET,
    )(grad, named, hot, dec)


def grad_block(core, operands):
    xq, gq, dpre, code, grad = operands
    nx, _, rows, toks = xq.shape
    lat, wide = dpre.shape[0], grad.shape[0]
    cols = 2 * lat + wide

    def body(core_ref, x_ref, g_ref, dpre_ref, code_ref, grad_ref, out_ref):
        core_at = core_ref[0]

        def put(a, b, lo, hi):
            part = lax.dot_general(a, b, (((1,), (1,)), ((), ())), preferred_element_type=f32)
            part = part.reshape(nx, rows, hi - lo)
            out_ref[:, :, lo:hi] = part.astype(bf16)

        x = x_ref[:, core_at].reshape(nx * rows, toks)
        put(x, grad_ref[...], 2 * lat, cols)
        put(x, dpre_ref[...], 0, lat)
        g = g_ref[:, core_at].reshape(nx * rows, toks)
        put(g, code_ref[...], lat, 2 * lat)

    vmem = pl.BlockSpec(memory_space=pltpu.VMEM)
    return pl.pallas_call(
        body,
        in_specs=[pl.BlockSpec(memory_space=pltpu.SMEM)] + [vmem] * 5,
        out_specs=vmem,
        out_shape=jax.ShapeDtypeStruct((nx, rows, cols), bf16),
        interpret=INTERPRET,
    )(core.reshape(1).astype(jnp.int32), xq, gq, dpre, code, grad)


def local(
    inputs,
    target,
    enc_weight,
    enc_bias,
    dec_weight,
    dec_bias,
    skip_weight,
    block_ids,
    slot_lists,
    slot_counts,
):
    tok_rows, fd = inputs.shape
    ld = enc_weight.shape[1]
    nz, ny = lax.axis_size(Z), lax.axis_size("y")
    nx, nc = lax.axis_size("x"), lax.axis_size("core")
    nt = nx * nc
    zl = lax.axis_size("zl")
    nb = ld // BLK
    cap = slot_lists.shape[2]
    zi, yi, ci = lax.axis_index(Z), lax.axis_index("y"), lax.axis_index("core")
    scale = 1.0 / math.sqrt(tok_rows * nt)
    xt = inputs.T
    tt = target.T

    def gather_z(part):
        pair = lax.all_gather(part, "zl", axis=0, tiled=True)
        return lax.all_gather(pair, "zh", axis=0, tiled=True)

    def share_y(part):
        return lax.all_to_all(jnp.broadcast_to(part[None], (ny,) + part.shape), "y", 0, 0)

    xq = gather_z(xt)
    er = lax.all_to_all(enc_weight.reshape(nz, ny, fd, ld), "y", 1, 0).reshape(ny, nz * fd, ld)
    zc = nz // nc
    wt = lax.dynamic_slice_in_dim(skip_weight, ci * zc * ny * fd, zc * ny * fd, 0)
    wt = lax.all_to_all(wt.reshape(zc, ny, fd, fd), "y", 1, 0).reshape(ny, zc * fd, fd)
    wr = lax.all_gather(wt, "core").transpose(0, 1, 3, 2).reshape(nc, ny * fd, zc * fd)
    lt = ld // nt
    dt = lax.dynamic_slice_in_dim(dec_weight, lax.axis_index(TOK) * lt, lt, 0)
    dt = lax.all_to_all(dt.reshape(lt, nz, ny * fd).transpose(1, 0, 2), Z, 0, 0)
    dd = lax.all_gather(dt, TOK)
    blocks_t = block_ids.T
    slots = slot_lists[0].reshape(nz, ny, cap)
    counts = slot_counts[0].reshape(nz, ny)
    plan_l = pick_plan(
        lax.dynamic_index_in_dim(slots, yi, 1, keepdims=False),
        lax.dynamic_index_in_dim(counts, yi, 1, keepdims=False),
        blocks_t, tok_rows, nb,
    )
    plan_z = pick_plan(
        lax.dynamic_index_in_dim(slots, zi, 0, keepdims=False),
        lax.dynamic_index_in_dim(counts, zi, 0, keepdims=False),
        blocks_t, tok_rows, nb,
    )
    named_l = jnp.repeat(plan_l[1].astype(bf16), BLK, axis=1)
    xq, er, wr, hot_l, named_l, plan_z = lax.optimization_barrier((xq, er, wr, plan_l[0], named_l, plan_z))
    own_mask = lax.dynamic_index_in_dim(plan_z[1], yi, 0, keepdims=False)
    bias = jnp.sum(jnp.where(own_mask[:, None, :], enc_bias.reshape(nb, BLK)[:, :, None], 0.0), axis=0)
    pre_part = ein("yrl,rt->ylt", er, xq).astype(bf16)
    pre_slots = lax.all_to_all(compress(pre_part, plan_z), "y", 0, 0)
    pre = jnp.sum(pre_slots, axis=0) + bias
    value, slope = gelu_pair(pre)
    code = value.astype(bf16)
    codes_l = lax.all_to_all(jnp.broadcast_to(code[None], (nz,) + code.shape), Z, 0, 0)
    out_part = decode_slots(codes_l, named_l, hot_l, dd, wr, xq).reshape(ny, fd, tok_rows)
    out_part = lax.all_to_all(out_part, "y", 0, 0)
    err = jnp.sum(out_part.astype(f32), axis=0) + dec_bias[:, None] - tt.astype(f32)
    grad = (err * scale).astype(bf16)
    gq = gather_z(grad)
    gz = share_y(grad).reshape(ny * fd, tok_rows)
    back_slots = lax.all_to_all(back_to_slots(gz, named_l, hot_l, dd), Z, 0, 0)
    back = jnp.sum(back_slots.astype(f32), axis=0)
    dpre = (back * slope).astype(bf16)
    slots_z = share_y(jnp.concatenate([dpre, code], axis=0))
    dpre_z = expand(slots_z[:, :BLK], plan_z).reshape(ny * ld, tok_rows)
    code_z = expand(slots_z[:, BLK:], plan_z).reshape(ny * ld, tok_rows)
    blocks = (nx, nc, zl * fd, tok_rows)
    operands = (xq.reshape(blocks), gq.reshape(blocks), dpre_z, code_z, gz)
    theirs = grad_block(1 - ci, operands)
    got = lax.ppermute(theirs, "core", [(0, 1), (1, 0)])
    mine = grad_block(ci, operands)
    pair = (mine.astype(f32) + got.astype(f32)).astype(bf16)
    total = jnp.sum(lax.all_to_all(pair, "x", 0, 0).astype(f32), axis=0).astype(bf16)
    lat = ny * ld

    def by_owner(total):
        return total.reshape(zl * fd, ny, total.shape[1] // ny)

    joint = jnp.concatenate(
        [by_owner(total[:, :lat]), by_owner(total[:, lat : 2 * lat]), by_owner(total[:, 2 * lat :])], axis=2
    )
    mine = lax.all_to_all(joint.transpose(1, 0, 2), "y", 0, 0).reshape(ny, zl, fd, 2 * ld + fd)
    mine = mine.transpose(1, 0, 2, 3).reshape(zl * ny * fd, 2 * ld + fd).astype(f32)
    grad_enc, grad_dec, grad_skip = mine[:, :ld], mine[:, ld : 2 * ld].T, mine[:, 2 * ld :]
    return (grad_enc, grad_dec, grad_skip)


def solution(mesh):
    nt, nd = mesh.devices.shape
    shape = (nt // 2, 2, nt, nd // NY // nt, NY)
    grid = Mesh(mesh.devices.reshape(shape), ("x", "core", "zh", "zl", "y"))
    in_specs = (
        P(TOK, DICT),
        P(TOK, DICT),
        P(None, DICT),
        P(DICT),
        P(DICT, None),
        P(DICT),
        P(None, DICT),
        P(TOK, None),
        P(TOK, None, None),
        P(TOK, None),
    )
    out_specs = (P(TOK, DICT), P(DICT, TOK), P(TOK, DICT))
    return jax.shard_map(local, mesh=grid, in_specs=in_specs, out_specs=out_specs, check_vma=False)
```

```python
import math

import jax
import jax.numpy as jnp
from jax import lax
from jax.experimental import pallas as pl
from jax.experimental.pallas import tpu as pltpu
from jax.sharding import Mesh
from jax.sharding import PartitionSpec as P

BLK = 16
NY = 4
INTERPRET = False
TOK = ("x", "core")
Z = ("zh", "zl")
DICT = ("zh", "zl", "y")
bf16 = jnp.bfloat16
f32 = jnp.float32


def gelu_pair(pre):
    factor = math.sqrt(2.0 / math.pi)
    inner = jnp.tanh(factor * (pre + 0.044715 * pre * pre * pre))
    value = 0.5 * pre * (1.0 + inner)
    slope = 0.5 * (1.0 + inner) + 0.5 * pre * (1.0 - inner * inner) * factor * (
        1.0 + 3.0 * 0.044715 * pre * pre
    )
    return (value, slope)


def ein(spec, a, b):
    return jnp.einsum(spec, a, b, preferred_element_type=f32)


def pick_plan(slots, counts, blocks_t, tok_rows, nb):
    per_token = blocks_t.shape[0]
    cap = slots.shape[1]
    token = slots // per_token
    hot = (token[:, :, None] == jnp.arange(tok_rows, dtype=jnp.int32)).astype(bf16)
    named = ein("rt,nst->nrs", (blocks_t % nb).astype(bf16), hot)
    rank = (slots % per_token)[:, None, :] == jnp.arange(per_token, dtype=jnp.int32)[None, :, None]
    block = jnp.sum(jnp.where(rank, named, 0.0), axis=1)
    valid = jnp.arange(cap, dtype=jnp.int32)[None, :] < counts[:, None]
    mask = (block[:, None, :] == jnp.arange(nb, dtype=f32)[None, :, None]) & valid[:, None, :]
    return hot, mask


def compress(part, plan):
    hot, mask = plan
    n, nb, cap = mask.shape
    rows = ein("nlt,nst->nls", part, hot).reshape(n, nb, BLK, cap)
    return jnp.sum(jnp.where(mask[:, :, None, :], rows, 0.0), axis=1)


def expand(slot_vals, plan):
    hot, mask = plan
    n, nb, cap = mask.shape
    rows = jnp.where(mask[:, :, None, :], slot_vals[:, None, :, :], jnp.zeros((), bf16))
    return ein("nls,nst->nlt", rows.reshape(n, nb * BLK, cap), hot).astype(bf16)


def contract(a, b, dim_a, dim_b):
    return lax.dot_general(a, b, (((dim_a,), (dim_b,)), ((), ())), preferred_element_type=f32)


def decode_slots(codes, named, hot, dec, skip, feats):
    n, lat, cap = named.shape
    toks, wide = hot.shape[2], dec.shape[3]
    parts, _, rows = skip.shape

    def body(codes_ref, named_ref, hot_ref, dec_ref, skip_ref, feats_ref, out_ref, slots_ref):
        for z in range(n):
            code = jnp.concatenate([codes_ref[z]] * (lat // BLK), axis=0) * named_ref[z]
            slots_ref[z] = contract(code, dec_ref[:, z].reshape(lat, wide), 0, 0).astype(bf16)
        total = contract(slots_ref[...].reshape(n * cap, wide), hot_ref[...].reshape(n * cap, toks), 0, 0)
        for k in range(parts):
            total = total + contract(skip_ref[k], feats_ref[k * rows : (k + 1) * rows], 1, 0)
        out_ref[...] = total.astype(bf16)

    vmem = pl.BlockSpec(memory_space=pltpu.VMEM)
    return pl.pallas_call(
        body,
        in_specs=[vmem] * 6,
        out_specs=vmem,
        out_shape=jax.ShapeDtypeStruct((wide, toks), bf16),
        scratch_shapes=[pltpu.VMEM((n, cap, wide), bf16)],
        interpret=INTERPRET,
    )(codes, named, hot, dec, skip, feats)


def back_to_slots(grad, named, hot, dec):
    n, lat, cap = named.shape
    toks, wide = hot.shape[2], dec.shape[3]

    def body(grad_ref, named_ref, hot_ref, dec_ref, out_ref):
        picked = contract(hot_ref[...].reshape(n * cap, toks), grad_ref[...], 1, 1).astype(bf16)
        for z in range(n):
            rows = contract(dec_ref[:, z].reshape(lat, wide), picked[z * cap : (z + 1) * cap], 1, 1)
            rows = rows * named_ref[z].astype(f32)
            total = rows[:BLK]
            for b in range(1, lat // BLK):
                total = total + rows[b * BLK : (b + 1) * BLK]
            out_ref[z] = total.astype(bf16)

    vmem = pl.BlockSpec(memory_space=pltpu.VMEM)
    return pl.pallas_call(
        body,
        in_specs=[vmem] * 4,
        out_specs=vmem,
        out_shape=jax.ShapeDtypeStruct((n, BLK, cap), bf16),
        interpret=INTERPRET,
    )(grad, named, hot, dec)


def grad_block(place, operands):
    xq, gq, dpre, code, grad = operands
    nx, _, rows, toks = xq.shape
    lat, wide = dpre.shape[0], grad.shape[0]
    cols = 2 * lat + wide

    def body(place_ref, x_ref, g_ref, dpre_ref, code_ref, grad_ref, out_ref):
        first, core_at = place_ref[0], place_ref[1]

        def put(a, b, lo, hi):
            out_ref[:, :, lo:hi] = contract(a, b, 1, 1).astype(bf16).reshape(nx, rows, hi - lo)

        def load(ref):
            return jnp.concatenate([ref[lax.rem(first + r, nx), core_at] for r in range(nx)], axis=0)

        x = load(x_ref)
        put(x, grad_ref[...], 2 * lat, cols)
        put(x, dpre_ref[...], 0, lat)
        put(load(g_ref), code_ref[...], lat, 2 * lat)

    vmem = pl.BlockSpec(memory_space=pltpu.VMEM)
    return pl.pallas_call(
        body,
        in_specs=[pl.BlockSpec(memory_space=pltpu.SMEM)] + [vmem] * 5,
        out_specs=vmem,
        out_shape=jax.ShapeDtypeStruct((nx, rows, cols), bf16),
        interpret=INTERPRET,
    )(place, xq, gq, dpre, code, grad)


def local(
    inputs,
    target,
    enc_weight,
    enc_bias,
    dec_weight,
    dec_bias,
    skip_weight,
    block_ids,
    slot_lists,
    slot_counts,
):
    tok_rows, fd = inputs.shape
    ld = enc_weight.shape[1]
    nz, ny = lax.axis_size(Z), lax.axis_size("y")
    nx, nc = lax.axis_size("x"), lax.axis_size("core")
    nt = nx * nc
    zl = lax.axis_size("zl")
    nb = ld // BLK
    cap = slot_lists.shape[2]
    zi, yi, ci = lax.axis_index(Z), lax.axis_index("y"), lax.axis_index("core")
    scale = 1.0 / math.sqrt(tok_rows * nt)
    xt = inputs.T
    tt = target.T

    def gather_z(part):
        pair = lax.all_gather(part, "zl", axis=0, tiled=True)
        return lax.all_gather(pair, "zh", axis=0, tiled=True)

    def share_y(part):
        return lax.all_to_all(jnp.broadcast_to(part[None], (ny,) + part.shape), "y", 0, 0)

    xq = gather_z(xt)
    er = lax.all_to_all(enc_weight.reshape(nz, ny, fd, ld), "y", 1, 0).reshape(ny, nz * fd, ld)
    zc = nz // nc
    wt = lax.dynamic_slice_in_dim(skip_weight, ci * zc * ny * fd, zc * ny * fd, 0)
    wt = lax.all_to_all(wt.reshape(zc, ny, fd, fd), "y", 1, 0).reshape(ny, zc * fd, fd)
    wr = lax.all_gather(wt, "core").transpose(0, 1, 3, 2).reshape(nc, ny * fd, zc * fd)
    lt = ld // nt
    dt = lax.dynamic_slice_in_dim(dec_weight, lax.axis_index(TOK) * lt, lt, 0)
    dt = lax.all_to_all(dt.reshape(lt, nz, ny * fd).transpose(1, 0, 2), Z, 0, 0)
    dd = lax.all_gather(dt, TOK)
    blocks_t = block_ids.T
    slots = slot_lists[0].reshape(nz, ny, cap)
    counts = slot_counts[0].reshape(nz, ny)
    plan_l = pick_plan(
        lax.dynamic_index_in_dim(slots, yi, 1, keepdims=False),
        lax.dynamic_index_in_dim(counts, yi, 1, keepdims=False),
        blocks_t, tok_rows, nb,
    )
    plan_z = pick_plan(
        lax.dynamic_index_in_dim(slots, zi, 0, keepdims=False),
        lax.dynamic_index_in_dim(counts, zi, 0, keepdims=False),
        blocks_t, tok_rows, nb,
    )
    named_l = jnp.repeat(plan_l[1].astype(bf16), BLK, axis=1)
    xq, er, wr, hot_l, named_l, plan_z = lax.optimization_barrier((xq, er, wr, plan_l[0], named_l, plan_z))
    own_mask = lax.dynamic_index_in_dim(plan_z[1], yi, 0, keepdims=False)
    bias = jnp.sum(jnp.where(own_mask[:, None, :], enc_bias.reshape(nb, BLK)[:, :, None], 0.0), axis=0)
    pre_part = ein("yrl,rt->ylt", er, xq).astype(bf16)
    pre_slots = lax.all_to_all(compress(pre_part, plan_z), "y", 0, 0)
    pre = jnp.sum(pre_slots, axis=0) + bias
    value, slope = gelu_pair(pre)
    code = value.astype(bf16)
    codes_l = lax.all_to_all(jnp.broadcast_to(code[None], (nz,) + code.shape), Z, 0, 0)
    out_part = decode_slots(codes_l, named_l, hot_l, dd, wr, xq).reshape(ny, fd, tok_rows)
    out_part = lax.all_to_all(out_part, "y", 0, 0)
    err = jnp.sum(out_part.astype(f32), axis=0) + dec_bias[:, None] - tt.astype(f32)
    grad = (err * scale).astype(bf16)
    gq = gather_z(grad)
    gz = share_y(grad).reshape(ny * fd, tok_rows)
    back_slots = lax.all_to_all(back_to_slots(gz, named_l, hot_l, dd), Z, 0, 0)
    back = jnp.sum(back_slots.astype(f32), axis=0)
    dpre = (back * slope).astype(bf16)
    slots_z = share_y(jnp.concatenate([dpre, code], axis=0))
    dpre_z = expand(slots_z[:, :BLK], plan_z).reshape(ny * ld, tok_rows)
    code_z = expand(slots_z[:, BLK:], plan_z).reshape(ny * ld, tok_rows)
    blocks = (nx, nc, zl * fd, tok_rows)
    operands = (xq.reshape(blocks), gq.reshape(blocks), dpre_z, code_z, gz)
    lat = ny * ld
    xi = lax.axis_index("x")
    theirs = grad_block(jnp.stack([xi, 1 - ci]).astype(jnp.int32), operands)
    got = lax.ppermute(theirs, "core", [(0, 1), (1, 0)])
    mine = grad_block(jnp.stack([xi, ci]).astype(jnp.int32), operands)
    own, right, far, left = [mine[r].astype(f32) + got[r].astype(f32) for r in range(4)]

    def up(a):
        return lax.ppermute(a.astype(bf16), "x", [(i, (i + 1) % nx) for i in range(nx)]).astype(f32)

    def down(a):
        return lax.ppermute(a.astype(bf16), "x", [(i, (i - 1) % nx) for i in range(nx)]).astype(f32)

    mid = lat + ld
    from_low, from_high = up(far[:, :mid]), down(far[:, mid:])
    right = jnp.concatenate([right[:, :mid] + from_low, right[:, mid:]], axis=1)
    left = jnp.concatenate([left[:, :mid], left[:, mid:] + from_high], axis=1)
    total = (own + up(right) + down(left)).astype(bf16)

    def by_owner(total):
        return total.reshape(zl * fd, ny, total.shape[1] // ny)

    joint = jnp.concatenate(
        [by_owner(total[:, :lat]), by_owner(total[:, lat : 2 * lat]), by_owner(total[:, 2 * lat :])], axis=2
    )
    mine = lax.all_to_all(joint.transpose(1, 0, 2), "y", 0, 0).reshape(ny, zl, fd, 2 * ld + fd)
    mine = mine.transpose(1, 0, 2, 3).reshape(zl * ny * fd, 2 * ld + fd).astype(f32)
    grad_enc, grad_dec, grad_skip = mine[:, :ld], mine[:, ld : 2 * ld].T, mine[:, 2 * ld :]
    return (grad_enc, grad_dec, grad_skip)


def solution(mesh):
    nt, nd = mesh.devices.shape
    shape = (nt // 2, 2, nt, nd // NY // nt, NY)
    grid = Mesh(mesh.devices.reshape(shape), ("x", "core", "zh", "zl", "y"))
    in_specs = (
        P(TOK, DICT),
        P(TOK, DICT),
        P(None, DICT),
        P(DICT),
        P(DICT, None),
        P(DICT),
        P(None, DICT),
        P(TOK, None),
        P(TOK, None, None),
        P(TOK, None),
    )
    out_specs = (P(TOK, DICT), P(DICT, TOK), P(TOK, DICT))
    return jax.shard_map(local, mesh=grid, in_specs=in_specs, out_specs=out_specs, check_vma=False)
```

```python
import math

import jax
import jax.numpy as jnp
from jax import lax
from jax.experimental import pallas as pl
from jax.experimental.pallas import tpu as pltpu
from jax.sharding import Mesh
from jax.sharding import PartitionSpec as P

BLK = 16
NY = 4
INTERPRET = False
TOK = ("x", "core")
Z = ("zh", "zl")
DICT = ("zh", "zl", "y")
bf16 = jnp.bfloat16
f32 = jnp.float32


def gelu_pair(pre):
    factor = math.sqrt(2.0 / math.pi)
    inner = jnp.tanh(factor * (pre + 0.044715 * pre * pre * pre))
    value = 0.5 * pre * (1.0 + inner)
    slope = 0.5 * (1.0 + inner) + 0.5 * pre * (1.0 - inner * inner) * factor * (
        1.0 + 3.0 * 0.044715 * pre * pre
    )
    return (value, slope)


def ein(spec, a, b):
    return jnp.einsum(spec, a, b, preferred_element_type=f32)


def pick_plan(slots, counts, blocks_t, tok_rows, nb):
    per_token = blocks_t.shape[0]
    cap = slots.shape[1]
    token = slots // per_token
    hot = (token[:, :, None] == jnp.arange(tok_rows, dtype=jnp.int32)).astype(bf16)
    named = ein("rt,nst->nrs", (blocks_t % nb).astype(bf16), hot)
    rank = (slots % per_token)[:, None, :] == jnp.arange(per_token, dtype=jnp.int32)[None, :, None]
    block = jnp.sum(jnp.where(rank, named, 0.0), axis=1)
    valid = jnp.arange(cap, dtype=jnp.int32)[None, :] < counts[:, None]
    mask = (block[:, None, :] == jnp.arange(nb, dtype=f32)[None, :, None]) & valid[:, None, :]
    return hot, mask


def compress(part, plan):
    hot, mask = plan
    n, nb, cap = mask.shape
    rows = ein("nlt,nst->nls", part, hot).reshape(n, nb, BLK, cap)
    return jnp.sum(jnp.where(mask[:, :, None, :], rows, 0.0), axis=1)


def expand(slot_vals, plan):
    hot, mask = plan
    n, nb, cap = mask.shape
    rows = jnp.where(mask[:, :, None, :], slot_vals[:, None, :, :], jnp.zeros((), bf16))
    return ein("nls,nst->nlt", rows.reshape(n, nb * BLK, cap), hot).astype(bf16)


def contract(a, b, dim_a, dim_b):
    return lax.dot_general(a, b, (((dim_a,), (dim_b,)), ((), ())), preferred_element_type=f32)


def decode_slots(codes, named, hot, dec, skip, feats):
    n, lat, cap = named.shape
    toks, wide = hot.shape[2], dec.shape[3]
    parts, _, rows = skip.shape

    def body(codes_ref, named_ref, hot_ref, dec_ref, skip_ref, feats_ref, out_ref, slots_ref):
        for z in range(n):
            code = jnp.concatenate([codes_ref[z]] * (lat // BLK), axis=0) * named_ref[z]
            slots_ref[z] = contract(code, dec_ref[:, z].reshape(lat, wide), 0, 0).astype(bf16)
        total = contract(slots_ref[...].reshape(n * cap, wide), hot_ref[...].reshape(n * cap, toks), 0, 0)
        for k in range(parts):
            total = total + contract(skip_ref[k], feats_ref[k * rows : (k + 1) * rows], 1, 0)
        out_ref[...] = total.astype(bf16)

    vmem = pl.BlockSpec(memory_space=pltpu.VMEM)
    return pl.pallas_call(
        body,
        in_specs=[vmem] * 6,
        out_specs=vmem,
        out_shape=jax.ShapeDtypeStruct((wide, toks), bf16),
        scratch_shapes=[pltpu.VMEM((n, cap, wide), bf16)],
        interpret=INTERPRET,
    )(codes, named, hot, dec, skip, feats)


def back_to_slots(grad, named, hot, dec):
    n, lat, cap = named.shape
    toks, wide = hot.shape[2], dec.shape[3]

    def body(grad_ref, named_ref, hot_ref, dec_ref, out_ref):
        picked = contract(hot_ref[...].reshape(n * cap, toks), grad_ref[...], 1, 1).astype(bf16)
        for z in range(n):
            rows = contract(dec_ref[:, z].reshape(lat, wide), picked[z * cap : (z + 1) * cap], 1, 1)
            rows = rows * named_ref[z].astype(f32)
            total = rows[:BLK]
            for b in range(1, lat // BLK):
                total = total + rows[b * BLK : (b + 1) * BLK]
            out_ref[z] = total.astype(bf16)

    vmem = pl.BlockSpec(memory_space=pltpu.VMEM)
    return pl.pallas_call(
        body,
        in_specs=[vmem] * 4,
        out_specs=vmem,
        out_shape=jax.ShapeDtypeStruct((n, BLK, cap), bf16),
        interpret=INTERPRET,
    )(grad, named, hot, dec)


def grad_block(core, pairs):
    nx, _, rows, toks = pairs[0][0].shape
    cols = sum(b.shape[0] for _, b in pairs)
    count = len(pairs)

    def body(core_ref, *refs):
        core_at, out_ref, lo = core_ref[0], refs[-1], 0
        for a_ref, b_ref in zip(refs[:count], refs[count:]):
            hi = lo + b_ref.shape[0]
            part = contract(a_ref[:, core_at].reshape(nx * rows, toks), b_ref[...], 1, 1)
            out_ref[:, :, lo:hi] = part.astype(bf16).reshape(nx, rows, hi - lo)
            lo = hi

    vmem = pl.BlockSpec(memory_space=pltpu.VMEM)
    return pl.pallas_call(
        body,
        in_specs=[pl.BlockSpec(memory_space=pltpu.SMEM)] + [vmem] * (2 * count),
        out_specs=vmem,
        out_shape=jax.ShapeDtypeStruct((nx, rows, cols), bf16),
        interpret=INTERPRET,
    )(core.reshape(1).astype(jnp.int32), *[a for a, _ in pairs], *[b for _, b in pairs])


def local(
    inputs,
    target,
    enc_weight,
    enc_bias,
    dec_weight,
    dec_bias,
    skip_weight,
    block_ids,
    slot_lists,
    slot_counts,
):
    tok_rows, fd = inputs.shape
    ld = enc_weight.shape[1]
    nz, ny = lax.axis_size(Z), lax.axis_size("y")
    nx, nc = lax.axis_size("x"), lax.axis_size("core")
    nt = nx * nc
    zl = lax.axis_size("zl")
    nb = ld // BLK
    cap = slot_lists.shape[2]
    zi, yi, ci = lax.axis_index(Z), lax.axis_index("y"), lax.axis_index("core")
    scale = 1.0 / math.sqrt(tok_rows * nt)
    xt = inputs.T
    tt = target.T

    def gather_z(part):
        pair = lax.all_gather(part, "zl", axis=0, tiled=True)
        return lax.all_gather(pair, "zh", axis=0, tiled=True)

    def share_y(part):
        return lax.all_to_all(jnp.broadcast_to(part[None], (ny,) + part.shape), "y", 0, 0)

    xq = gather_z(xt)
    er = lax.all_to_all(enc_weight.reshape(nz, ny, fd, ld), "y", 1, 0).reshape(ny, nz * fd, ld)
    zc = nz // nc
    wt = lax.dynamic_slice_in_dim(skip_weight, ci * zc * ny * fd, zc * ny * fd, 0)
    wt = lax.all_to_all(wt.reshape(zc, ny, fd, fd), "y", 1, 0).reshape(ny, zc * fd, fd)
    wr = lax.all_gather(wt, "core").transpose(0, 1, 3, 2).reshape(nc, ny * fd, zc * fd)
    lt = ld // nt
    dt = lax.dynamic_slice_in_dim(dec_weight, lax.axis_index(TOK) * lt, lt, 0)
    dt = lax.all_to_all(dt.reshape(lt, nz, ny * fd).transpose(1, 0, 2), Z, 0, 0)
    dd = lax.all_gather(dt, TOK)
    blocks_t = block_ids.T
    slots = slot_lists[0].reshape(nz, ny, cap)
    counts = slot_counts[0].reshape(nz, ny)
    plan_l = pick_plan(
        lax.dynamic_index_in_dim(slots, yi, 1, keepdims=False),
        lax.dynamic_index_in_dim(counts, yi, 1, keepdims=False),
        blocks_t, tok_rows, nb,
    )
    plan_z = pick_plan(
        lax.dynamic_index_in_dim(slots, zi, 0, keepdims=False),
        lax.dynamic_index_in_dim(counts, zi, 0, keepdims=False),
        blocks_t, tok_rows, nb,
    )
    named_l = jnp.repeat(plan_l[1].astype(bf16), BLK, axis=1)
    xq, er, wr, hot_l, named_l, plan_z = lax.optimization_barrier((xq, er, wr, plan_l[0], named_l, plan_z))
    own_mask = lax.dynamic_index_in_dim(plan_z[1], yi, 0, keepdims=False)
    bias = jnp.sum(jnp.where(own_mask[:, None, :], enc_bias.reshape(nb, BLK)[:, :, None], 0.0), axis=0)
    pre_part = ein("yrl,rt->ylt", er, xq).astype(bf16)
    pre_slots = lax.all_to_all(compress(pre_part, plan_z), "y", 0, 0)
    pre = jnp.sum(pre_slots, axis=0) + bias
    value, slope = gelu_pair(pre)
    code = value.astype(bf16)
    code_pair = lax.all_gather(code, "zl")
    nzh = nz // zl
    codes_l = lax.all_to_all(jnp.broadcast_to(code_pair[None], (nzh,) + code_pair.shape), "zh", 0, 0)
    codes_l = codes_l.reshape(nz, BLK, cap)
    out_part = decode_slots(codes_l, named_l, hot_l, dd, wr, xq).reshape(ny, fd, tok_rows)
    out_part = lax.all_to_all(out_part, "y", 0, 0)
    err = jnp.sum(out_part.astype(f32), axis=0) + dec_bias[:, None] - tt.astype(f32)
    grad = (err * scale).astype(bf16)
    gq = gather_z(grad)
    gz = share_y(grad).reshape(ny * fd, tok_rows)
    back_slots = back_to_slots(gz, named_l, hot_l, dd).reshape(nzh, zl, BLK, cap)
    back_pair = jnp.sum(lax.all_to_all(back_slots, "zh", 0, 0).astype(f32), axis=0)
    back = jnp.sum(lax.all_to_all(back_pair, "zl", 0, 0), axis=0)
    dpre = (back * slope).astype(bf16)
    slots_z = share_y(jnp.concatenate([dpre, code], axis=0))
    dpre_z = expand(slots_z[:, :BLK], plan_z).reshape(ny * ld, tok_rows)
    code_z = expand(slots_z[:, BLK:], plan_z).reshape(ny * ld, tok_rows)
    blocks = (nx, nc, zl * fd, tok_rows)

    def pair_sum(pairs):
        got = lax.ppermute(grad_block(1 - ci, pairs), "core", [(0, 1), (1, 0)])
        return (grad_block(ci, pairs).astype(f32) + got.astype(f32)).astype(bf16)

    xb = xq.reshape(blocks)
    enc_pair = pair_sum([(xb, dpre_z)])
    gq, enc_pair, code_z = lax.optimization_barrier((gq, enc_pair, code_z))
    enc_total = lax.psum_scatter(enc_pair.reshape(nx * zl * fd, ny * ld), "x", scatter_dimension=0, tiled=True)
    rest_pair = pair_sum([(gq.reshape(blocks), code_z), (xb, gz)])
    rest = jnp.sum(lax.all_to_all(rest_pair, "x", 0, 0).astype(f32), axis=0).astype(bf16)
    lat = ny * ld

    def by_owner(total):
        return total.reshape(zl * fd, ny, total.shape[1] // ny)

    joint = jnp.concatenate(
        [by_owner(enc_total), by_owner(rest[:, :lat]), by_owner(rest[:, lat:])], axis=2
    )
    mine = lax.all_to_all(joint.transpose(1, 0, 2), "y", 0, 0).reshape(ny, zl, fd, 2 * ld + fd)
    mine = mine.transpose(1, 0, 2, 3).reshape(zl * ny * fd, 2 * ld + fd).astype(f32)
    grad_enc, grad_dec, grad_skip = mine[:, :ld], mine[:, ld : 2 * ld].T, mine[:, 2 * ld :]
    return (grad_enc, grad_dec, grad_skip)


def solution(mesh):
    nt, nd = mesh.devices.shape
    shape = (nt // 2, 2, nt, nd // NY // nt, NY)
    grid = Mesh(mesh.devices.reshape(shape), ("x", "core", "zh", "zl", "y"))
    in_specs = (
        P(TOK, DICT),
        P(TOK, DICT),
        P(None, DICT),
        P(DICT),
        P(DICT, None),
        P(DICT),
        P(None, DICT),
        P(TOK, None),
        P(TOK, None, None),
        P(TOK, None),
    )
    out_specs = (P(TOK, DICT), P(DICT, TOK), P(TOK, DICT))
    return jax.shard_map(local, mesh=grid, in_specs=in_specs, out_specs=out_specs, check_vma=False)
```

```python
import math

import jax
import jax.numpy as jnp
from jax import lax
from jax.experimental import pallas as pl
from jax.experimental.pallas import tpu as pltpu
from jax.sharding import Mesh
from jax.sharding import PartitionSpec as P

BLK = 16
NY = 4
INTERPRET = False
TOK = ("x", "core")
Z = ("zh", "zl")
DICT = ("zh", "zl", "y")
bf16 = jnp.bfloat16
f32 = jnp.float32


def gelu_pair(pre):
    factor = math.sqrt(2.0 / math.pi)
    inner = jnp.tanh(factor * (pre + 0.044715 * pre * pre * pre))
    value = 0.5 * pre * (1.0 + inner)
    slope = 0.5 * (1.0 + inner) + 0.5 * pre * (1.0 - inner * inner) * factor * (
        1.0 + 3.0 * 0.044715 * pre * pre
    )
    return (value, slope)


def ein(spec, a, b):
    return jnp.einsum(spec, a, b, preferred_element_type=f32)


def pick_plan(slots, counts, blocks_t, tok_rows, nb):
    per_token = blocks_t.shape[0]
    cap = slots.shape[1]
    token = slots // per_token
    hot = (token[:, :, None] == jnp.arange(tok_rows, dtype=jnp.int32)).astype(bf16)
    named = ein("rt,nst->nrs", (blocks_t % nb).astype(bf16), hot)
    rank = (slots % per_token)[:, None, :] == jnp.arange(per_token, dtype=jnp.int32)[None, :, None]
    block = jnp.sum(jnp.where(rank, named, 0.0), axis=1)
    valid = jnp.arange(cap, dtype=jnp.int32)[None, :] < counts[:, None]
    mask = (block[:, None, :] == jnp.arange(nb, dtype=f32)[None, :, None]) & valid[:, None, :]
    return hot, mask


def compress(part, plan):
    hot, mask = plan
    n, nb, cap = mask.shape
    rows = ein("nlt,nst->nls", part, hot).reshape(n, nb, BLK, cap)
    return jnp.sum(jnp.where(mask[:, :, None, :], rows, 0.0), axis=1)


def expand(slot_vals, plan):
    hot, mask = plan
    n, nb, cap = mask.shape
    rows = jnp.where(mask[:, :, None, :], slot_vals[:, None, :, :], jnp.zeros((), bf16))
    return ein("nls,nst->nlt", rows.reshape(n, nb * BLK, cap), hot).astype(bf16)


def contract(a, b, dim_a, dim_b):
    return lax.dot_general(a, b, (((dim_a,), (dim_b,)), ((), ())), preferred_element_type=f32)


def decode_slots(codes, named, hot, dec, skip, feats):
    n, lat, cap = named.shape
    toks, wide = hot.shape[2], dec.shape[3]
    parts, _, rows = skip.shape

    def body(codes_ref, named_ref, hot_ref, dec_ref, skip_ref, feats_ref, out_ref, slots_ref):
        for z in range(n):
            code = jnp.concatenate([codes_ref[z]] * (lat // BLK), axis=0) * named_ref[z]
            slots_ref[z] = contract(code, dec_ref[:, z].reshape(lat, wide), 0, 0).astype(bf16)
        total = contract(slots_ref[...].reshape(n * cap, wide), hot_ref[...].reshape(n * cap, toks), 0, 0)
        for k in range(parts):
            total = total + contract(skip_ref[k], feats_ref[k * rows : (k + 1) * rows], 1, 0)
        out_ref[...] = total.astype(bf16)

    vmem = pl.BlockSpec(memory_space=pltpu.VMEM)
    return pl.pallas_call(
        body,
        in_specs=[vmem] * 6,
        out_specs=vmem,
        out_shape=jax.ShapeDtypeStruct((wide, toks), bf16),
        scratch_shapes=[pltpu.VMEM((n, cap, wide), bf16)],
        interpret=INTERPRET,
    )(codes, named, hot, dec, skip, feats)


def back_to_slots(grad, named, hot, dec):
    n, lat, cap = named.shape
    toks, wide = hot.shape[2], dec.shape[3]

    def body(grad_ref, named_ref, hot_ref, dec_ref, out_ref):
        picked = contract(hot_ref[...].reshape(n * cap, toks), grad_ref[...], 1, 1).astype(bf16)
        for z in range(n):
            rows = contract(dec_ref[:, z].reshape(lat, wide), picked[z * cap : (z + 1) * cap], 1, 1)
            rows = rows * named_ref[z].astype(f32)
            total = rows[:BLK]
            for b in range(1, lat // BLK):
                total = total + rows[b * BLK : (b + 1) * BLK]
            out_ref[z] = total.astype(bf16)

    vmem = pl.BlockSpec(memory_space=pltpu.VMEM)
    return pl.pallas_call(
        body,
        in_specs=[vmem] * 4,
        out_specs=vmem,
        out_shape=jax.ShapeDtypeStruct((n, BLK, cap), bf16),
        interpret=INTERPRET,
    )(grad, named, hot, dec)


def grad_block(core, pairs):
    nx, _, rows, toks = pairs[0][0].shape
    cols = sum(b.shape[0] for _, b in pairs)
    count = len(pairs)

    def body(core_ref, *refs):
        core_at, out_ref, lo = core_ref[0], refs[-1], 0
        for a_ref, b_ref in zip(refs[:count], refs[count:]):
            hi = lo + b_ref.shape[0]
            part = contract(a_ref[:, core_at].reshape(nx * rows, toks), b_ref[...], 1, 1)
            out_ref[:, :, lo:hi] = part.astype(bf16).reshape(nx, rows, hi - lo)
            lo = hi

    vmem = pl.BlockSpec(memory_space=pltpu.VMEM)
    return pl.pallas_call(
        body,
        in_specs=[pl.BlockSpec(memory_space=pltpu.SMEM)] + [vmem] * (2 * count),
        out_specs=vmem,
        out_shape=jax.ShapeDtypeStruct((nx, rows, cols), bf16),
        interpret=INTERPRET,
    )(core.reshape(1).astype(jnp.int32), *[a for a, _ in pairs], *[b for _, b in pairs])


def local(
    inputs,
    target,
    enc_weight,
    enc_bias,
    dec_weight,
    dec_bias,
    skip_weight,
    block_ids,
    slot_lists,
    slot_counts,
):
    tok_rows, fd = inputs.shape
    ld = enc_weight.shape[1]
    nz, ny = lax.axis_size(Z), lax.axis_size("y")
    nx, nc = lax.axis_size("x"), lax.axis_size("core")
    nt = nx * nc
    zl = lax.axis_size("zl")
    nb = ld // BLK
    cap = slot_lists.shape[2]
    zi, yi, ci = lax.axis_index(Z), lax.axis_index("y"), lax.axis_index("core")
    scale = 1.0 / math.sqrt(tok_rows * nt)
    xt = inputs.T
    tt = target.T

    def gather_z(part):
        pair = lax.all_gather(part, "zl", axis=0, tiled=True)
        return lax.all_gather(pair, "zh", axis=0, tiled=True)

    def share_y(part):
        return lax.all_to_all(jnp.broadcast_to(part[None], (ny,) + part.shape), "y", 0, 0)

    xq = gather_z(xt)
    er = lax.all_to_all(enc_weight.reshape(nz, ny, fd, ld), "y", 1, 0).reshape(ny, nz * fd, ld)
    zc = nz // nc
    wt = lax.dynamic_slice_in_dim(skip_weight, ci * zc * ny * fd, zc * ny * fd, 0)
    wt = lax.all_to_all(wt.reshape(zc, ny, fd, fd), "y", 1, 0).reshape(ny, zc * fd, fd)
    wr = lax.all_gather(wt, "core").transpose(0, 1, 3, 2).reshape(nc, ny * fd, zc * fd)
    lt = ld // nt
    dt = lax.dynamic_slice_in_dim(dec_weight, lax.axis_index(TOK) * lt, lt, 0)
    dt = lax.all_to_all(dt.reshape(lt, nz, ny * fd).transpose(1, 0, 2), Z, 0, 0)
    dd = lax.all_gather(dt, TOK)
    blocks_t = block_ids.T
    slots = slot_lists[0].reshape(nz, ny, cap)
    counts = slot_counts[0].reshape(nz, ny)
    plan_l = pick_plan(
        lax.dynamic_index_in_dim(slots, yi, 1, keepdims=False),
        lax.dynamic_index_in_dim(counts, yi, 1, keepdims=False),
        blocks_t, tok_rows, nb,
    )
    plan_z = pick_plan(
        lax.dynamic_index_in_dim(slots, zi, 0, keepdims=False),
        lax.dynamic_index_in_dim(counts, zi, 0, keepdims=False),
        blocks_t, tok_rows, nb,
    )
    named_l = jnp.repeat(plan_l[1].astype(bf16), BLK, axis=1)
    xq, er, wr, hot_l, named_l, plan_z = lax.optimization_barrier((xq, er, wr, plan_l[0], named_l, plan_z))
    own_mask = lax.dynamic_index_in_dim(plan_z[1], yi, 0, keepdims=False)
    bias = jnp.sum(jnp.where(own_mask[:, None, :], enc_bias.reshape(nb, BLK)[:, :, None], 0.0), axis=0)
    pre_part = ein("yrl,rt->ylt", er, xq).astype(bf16)
    pre_slots = lax.all_to_all(compress(pre_part, plan_z), "y", 0, 0)
    pre = jnp.sum(pre_slots, axis=0) + bias
    value, slope = gelu_pair(pre)
    code = value.astype(bf16)
    codes_l = lax.all_to_all(jnp.broadcast_to(code[None], (nz,) + code.shape), Z, 0, 0)
    out_part = decode_slots(codes_l, named_l, hot_l, dd, wr, xq).reshape(ny, fd, tok_rows)
    out_part = lax.all_to_all(out_part, "y", 0, 0)
    err = jnp.sum(out_part.astype(f32), axis=0) + dec_bias[:, None] - tt.astype(f32)
    grad = (err * scale).astype(bf16)
    gq = gather_z(grad)
    gz = share_y(grad).reshape(ny * fd, tok_rows)
    back_slots = lax.all_to_all(back_to_slots(gz, named_l, hot_l, dd), Z, 0, 0)
    back = jnp.sum(back_slots.astype(f32), axis=0)
    dpre = (back * slope).astype(bf16)
    slots_z = share_y(jnp.concatenate([dpre, code], axis=0))
    dpre_z = expand(slots_z[:, :BLK], plan_z).reshape(ny * ld, tok_rows)
    code_z = expand(slots_z[:, BLK:], plan_z).reshape(ny * ld, tok_rows)
    blocks = (nx, nc, zl * fd, tok_rows)

    def pair_sum(pairs):
        got = lax.ppermute(grad_block(1 - ci, pairs), "core", [(0, 1), (1, 0)])
        return (grad_block(ci, pairs).astype(f32) + got.astype(f32)).astype(bf16)

    xb = xq.reshape(blocks)
    early_pair = pair_sum([(xb, dpre_z), (xb, gz)])
    gq, early_pair, code_z = lax.optimization_barrier((gq, early_pair, code_z))
    early_pair = early_pair.reshape(nx * zl * fd, ny * (ld + fd))
    early = lax.psum_scatter(early_pair, "x", scatter_dimension=0, tiled=True)
    dec_pair = pair_sum([(gq.reshape(blocks), code_z)])
    dec = jnp.sum(lax.all_to_all(dec_pair, "x", 0, 0).astype(f32), axis=0).astype(bf16)
    lat = ny * ld

    def by_owner(total):
        return total.reshape(zl * fd, ny, total.shape[1] // ny)

    joint = jnp.concatenate(
        [by_owner(early[:, :lat]), by_owner(dec), by_owner(early[:, lat:])], axis=2
    )
    mine = lax.all_to_all(joint.transpose(1, 0, 2), "y", 0, 0).reshape(ny, zl, fd, 2 * ld + fd)
    mine = mine.transpose(1, 0, 2, 3).reshape(zl * ny * fd, 2 * ld + fd).astype(f32)
    grad_enc, grad_dec, grad_skip = mine[:, :ld], mine[:, ld : 2 * ld].T, mine[:, 2 * ld :]
    return (grad_enc, grad_dec, grad_skip)


def solution(mesh):
    nt, nd = mesh.devices.shape
    shape = (nt // 2, 2, nt, nd // NY // nt, NY)
    grid = Mesh(mesh.devices.reshape(shape), ("x", "core", "zh", "zl", "y"))
    in_specs = (
        P(TOK, DICT),
        P(TOK, DICT),
        P(None, DICT),
        P(DICT),
        P(DICT, None),
        P(DICT),
        P(None, DICT),
        P(TOK, None),
        P(TOK, None, None),
        P(TOK, None),
    )
    out_specs = (P(TOK, DICT), P(DICT, TOK), P(TOK, DICT))
    return jax.shard_map(local, mesh=grid, in_specs=in_specs, out_specs=out_specs, check_vma=False)
```

```python
import math

import jax
import jax.numpy as jnp
from jax import lax
from jax.experimental import pallas as pl
from jax.experimental.pallas import tpu as pltpu
from jax.sharding import Mesh
from jax.sharding import PartitionSpec as P

BLK = 16
NY = 4
INTERPRET = False
TOK = ("x", "core")
Z = ("zh", "zl")
DICT = ("zh", "zl", "y")
bf16 = jnp.bfloat16
f32 = jnp.float32


def gelu_pair(pre):
    factor = math.sqrt(2.0 / math.pi)
    inner = jnp.tanh(factor * (pre + 0.044715 * pre * pre * pre))
    value = 0.5 * pre * (1.0 + inner)
    slope = 0.5 * (1.0 + inner) + 0.5 * pre * (1.0 - inner * inner) * factor * (
        1.0 + 3.0 * 0.044715 * pre * pre
    )
    return (value, slope)


def ein(spec, a, b):
    return jnp.einsum(spec, a, b, preferred_element_type=f32)


def pick_plan(slots, counts, blocks_t, tok_rows, nb):
    per_token = blocks_t.shape[0]
    cap = slots.shape[1]
    token = slots // per_token
    hot = (token[:, :, None] == jnp.arange(tok_rows, dtype=jnp.int32)).astype(bf16)
    named = ein("rt,nst->nrs", (blocks_t % nb).astype(bf16), hot)
    rank = (slots % per_token)[:, None, :] == jnp.arange(per_token, dtype=jnp.int32)[None, :, None]
    block = jnp.sum(jnp.where(rank, named, 0.0), axis=1)
    valid = jnp.arange(cap, dtype=jnp.int32)[None, :] < counts[:, None]
    mask = (block[:, None, :] == jnp.arange(nb, dtype=f32)[None, :, None]) & valid[:, None, :]
    lanes = jnp.arange(nb * BLK, dtype=jnp.int32) // BLK
    named = (block[:, None, :] == lanes.astype(f32)[None, :, None]) & valid[:, None, :]
    return hot, mask, named.astype(bf16)


def compress(part, plan):
    hot, mask, _ = plan
    n, nb, cap = mask.shape
    rows = ein("nlt,nst->nls", part, hot).reshape(n, nb, BLK, cap)
    return jnp.sum(jnp.where(mask[:, :, None, :], rows, 0.0), axis=1)


def expand(slot_vals, plan):
    hot, mask, _ = plan
    n, nb, cap = mask.shape
    rows = jnp.where(mask[:, :, None, :], slot_vals[:, None, :, :], jnp.zeros((), bf16))
    return ein("nls,nst->nlt", rows.reshape(n, nb * BLK, cap), hot).astype(bf16)


def contract(a, b, dim_a, dim_b):
    return lax.dot_general(a, b, (((dim_a,), (dim_b,)), ((), ())), preferred_element_type=f32)


def decode_slots(codes, named, hot, dec, skip, feats):
    n, lat, cap = named.shape
    toks, wide = hot.shape[2], dec.shape[3]
    parts, _, rows = skip.shape

    def body(codes_ref, named_ref, hot_ref, dec_ref, skip_ref, feats_ref, out_ref, slots_ref):
        for z in range(n):
            code = jnp.concatenate([codes_ref[z]] * (lat // BLK), axis=0) * named_ref[z]
            slots_ref[z] = contract(code, dec_ref[:, z].reshape(lat, wide), 0, 0).astype(bf16)
        total = contract(slots_ref[...].reshape(n * cap, wide), hot_ref[...].reshape(n * cap, toks), 0, 0)
        for k in range(parts):
            total = total + contract(skip_ref[k], feats_ref[k * rows : (k + 1) * rows], 1, 0)
        out_ref[...] = total.astype(bf16)

    vmem = pl.BlockSpec(memory_space=pltpu.VMEM)
    return pl.pallas_call(
        body,
        in_specs=[vmem] * 6,
        out_specs=vmem,
        out_shape=jax.ShapeDtypeStruct((wide, toks), bf16),
        scratch_shapes=[pltpu.VMEM((n, cap, wide), bf16)],
        interpret=INTERPRET,
    )(codes, named, hot, dec, skip, feats)


def back_to_slots(grad, named, hot, dec):
    n, lat, cap = named.shape
    toks, wide = hot.shape[2], dec.shape[3]

    def body(grad_ref, named_ref, hot_ref, dec_ref, out_ref):
        picked = contract(hot_ref[...].reshape(n * cap, toks), grad_ref[...], 1, 1).astype(bf16)
        for z in range(n):
            rows = contract(dec_ref[:, z].reshape(lat, wide), picked[z * cap : (z + 1) * cap], 1, 1)
            rows = rows * named_ref[z].astype(f32)
            total = rows[:BLK]
            for b in range(1, lat // BLK):
                total = total + rows[b * BLK : (b + 1) * BLK]
            out_ref[z] = total.astype(bf16)

    vmem = pl.BlockSpec(memory_space=pltpu.VMEM)
    return pl.pallas_call(
        body,
        in_specs=[vmem] * 4,
        out_specs=vmem,
        out_shape=jax.ShapeDtypeStruct((n, BLK, cap), bf16),
        interpret=INTERPRET,
    )(grad, named, hot, dec)


def grad_block(core, pairs):
    nx, _, rows, toks = pairs[0][0].shape
    cols = sum(b.shape[0] for _, b in pairs)
    count = len(pairs)

    def body(core_ref, *refs):
        core_at, out_ref, lo = core_ref[0], refs[-1], 0
        for a_ref, b_ref in zip(refs[:count], refs[count:]):
            hi = lo + b_ref.shape[0]
            part = contract(a_ref[:, core_at].reshape(nx * rows, toks), b_ref[...], 1, 1)
            out_ref[:, :, lo:hi] = part.astype(bf16).reshape(nx, rows, hi - lo)
            lo = hi

    vmem = pl.BlockSpec(memory_space=pltpu.VMEM)
    return pl.pallas_call(
        body,
        in_specs=[pl.BlockSpec(memory_space=pltpu.SMEM)] + [vmem] * (2 * count),
        out_specs=vmem,
        out_shape=jax.ShapeDtypeStruct((nx, rows, cols), bf16),
        interpret=INTERPRET,
    )(core.reshape(1).astype(jnp.int32), *[a for a, _ in pairs], *[b for _, b in pairs])


def local(
    inputs,
    target,
    enc_weight,
    enc_bias,
    dec_weight,
    dec_bias,
    skip_weight,
    block_ids,
    slot_lists,
    slot_counts,
):
    tok_rows, fd = inputs.shape
    ld = enc_weight.shape[1]
    nz, ny = lax.axis_size(Z), lax.axis_size("y")
    nx, nc = lax.axis_size("x"), lax.axis_size("core")
    nt = nx * nc
    zl = lax.axis_size("zl")
    nb = ld // BLK
    cap = slot_lists.shape[2]
    zi, yi, ci = lax.axis_index(Z), lax.axis_index("y"), lax.axis_index("core")
    scale = 1.0 / math.sqrt(tok_rows * nt)
    xt = inputs.T
    tt = target.T

    def gather_z(part):
        pair = lax.all_gather(part, "zl", axis=0, tiled=True)
        return lax.all_gather(pair, "zh", axis=0, tiled=True)

    def share_y(part):
        return lax.all_to_all(jnp.broadcast_to(part[None], (ny,) + part.shape), "y", 0, 0)

    xq = gather_z(xt)
    er = lax.all_to_all(enc_weight.reshape(nz, ny, fd, ld), "y", 1, 0).reshape(ny, nz * fd, ld)
    zc = nz // nc
    wt = lax.dynamic_slice_in_dim(skip_weight, ci * zc * ny * fd, zc * ny * fd, 0)
    wt = lax.all_to_all(wt.reshape(zc, ny, fd, fd), "y", 1, 0).reshape(ny, zc * fd, fd)
    wr = lax.all_gather(wt, "core").transpose(0, 1, 3, 2).reshape(nc, ny * fd, zc * fd)
    lt = ld // nt
    dt = lax.dynamic_slice_in_dim(dec_weight, lax.axis_index(TOK) * lt, lt, 0)
    dt = lax.all_to_all(dt.reshape(lt, nz, ny * fd).transpose(1, 0, 2), Z, 0, 0)
    dd = lax.all_gather(dt, TOK)
    blocks_t = block_ids.T
    slots = slot_lists[0].reshape(nz, ny, cap)
    counts = slot_counts[0].reshape(nz, ny)
    plan_l = pick_plan(
        lax.dynamic_index_in_dim(slots, yi, 1, keepdims=False),
        lax.dynamic_index_in_dim(counts, yi, 1, keepdims=False),
        blocks_t, tok_rows, nb,
    )
    plan_z = pick_plan(
        lax.dynamic_index_in_dim(slots, zi, 0, keepdims=False),
        lax.dynamic_index_in_dim(counts, zi, 0, keepdims=False),
        blocks_t, tok_rows, nb,
    )
    xq, er, wr, hot_l, named_l, plan_z = lax.optimization_barrier((xq, er, wr, plan_l[0], plan_l[2], plan_z))
    own_mask = lax.dynamic_index_in_dim(plan_z[1], yi, 0, keepdims=False)
    bias = jnp.sum(jnp.where(own_mask[:, None, :], enc_bias.reshape(nb, BLK)[:, :, None], 0.0), axis=0)
    pre_part = ein("yrl,rt->ylt", er, xq).astype(bf16)
    pre_slots = lax.all_to_all(compress(pre_part, plan_z), "y", 0, 0)
    pre = jnp.sum(pre_slots, axis=0) + bias
    value, slope = gelu_pair(pre)
    code = value.astype(bf16)
    codes_l = lax.all_to_all(jnp.broadcast_to(code[None], (nz,) + code.shape), Z, 0, 0)
    out_part = decode_slots(codes_l, named_l, hot_l, dd, wr, xq).reshape(ny, fd, tok_rows)
    out_part = lax.all_to_all(out_part, "y", 0, 0)
    err = jnp.sum(out_part.astype(f32), axis=0) + dec_bias[:, None] - tt.astype(f32)
    grad = (err * scale).astype(bf16)
    gq = gather_z(grad)
    gz = share_y(grad).reshape(ny * fd, tok_rows)
    back_slots = lax.all_to_all(back_to_slots(gz, named_l, hot_l, dd), Z, 0, 0)
    back = jnp.sum(back_slots.astype(f32), axis=0)
    dpre = (back * slope).astype(bf16)
    slots_z = share_y(jnp.concatenate([dpre, code], axis=0))
    dpre_z = expand(slots_z[:, :BLK], plan_z).reshape(ny * ld, tok_rows)
    code_z = expand(slots_z[:, BLK:], plan_z).reshape(ny * ld, tok_rows)
    blocks = (nx, nc, zl * fd, tok_rows)

    def pair_sum(pairs):
        got = lax.ppermute(grad_block(1 - ci, pairs), "core", [(0, 1), (1, 0)])
        return (grad_block(ci, pairs).astype(f32) + got.astype(f32)).astype(bf16)

    xb = xq.reshape(blocks)
    early_pair = pair_sum([(xb, dpre_z), (xb, gz)])
    gq, early_pair, code_z = lax.optimization_barrier((gq, early_pair, code_z))
    early_pair = early_pair.reshape(nx * zl * fd, ny * (ld + fd))
    early = lax.psum_scatter(early_pair, "x", scatter_dimension=0, tiled=True)
    dec_pair = pair_sum([(gq.reshape(blocks), code_z)])
    dec = jnp.sum(lax.all_to_all(dec_pair, "x", 0, 0).astype(f32), axis=0).astype(bf16)
    lat = ny * ld

    def by_owner(total):
        return total.reshape(zl * fd, ny, total.shape[1] // ny)

    joint = jnp.concatenate(
        [by_owner(early[:, :lat]), by_owner(dec), by_owner(early[:, lat:])], axis=2
    )
    mine = lax.all_to_all(joint.transpose(1, 0, 2), "y", 0, 0).reshape(ny, zl, fd, 2 * ld + fd)
    mine = mine.transpose(1, 0, 2, 3).reshape(zl * ny * fd, 2 * ld + fd).astype(f32)
    grad_enc, grad_dec, grad_skip = mine[:, :ld], mine[:, ld : 2 * ld].T, mine[:, 2 * ld :]
    return (grad_enc, grad_dec, grad_skip)


def solution(mesh):
    nt, nd = mesh.devices.shape
    shape = (nt // 2, 2, nt, nd // NY // nt, NY)
    grid = Mesh(mesh.devices.reshape(shape), ("x", "core", "zh", "zl", "y"))
    in_specs = (
        P(TOK, DICT),
        P(TOK, DICT),
        P(None, DICT),
        P(DICT),
        P(DICT, None),
        P(DICT),
        P(None, DICT),
        P(TOK, None),
        P(TOK, None, None),
        P(TOK, None),
    )
    out_specs = (P(TOK, DICT), P(DICT, TOK), P(TOK, DICT))
    return jax.shard_map(local, mesh=grid, in_specs=in_specs, out_specs=out_specs, check_vma=False)
```
